32 devices in a mesh: clip: 2 (over x), wa: 4 (over y, core), ha: 4 (over z).
Axes of the slice: x: 2, y: 2, z: 4, core: 2. Of those that a mesh axis runs over, the one named last changes fastest.
Arguments:
- queries: bfloat16 [4, 32, 32, 1536], P('clip', 'ha', 'wa'), parts along dimension 0, may hold values from -7 to 7
- keys: bfloat16 [4, 32, 32, 1536], P('clip', 'ha', 'wa'), parts along dimension 0, may hold values from -7 to 7
- values: bfloat16 [4, 32, 32, 1536], P('clip', 'ha', 'wa'), parts along dimension 0, may hold values from -15 to 15
- out_grad: bfloat16 [4, 32, 32, 1536], P('clip', 'ha', 'wa'), parts along dimension 0, may hold values from -16 to 16
- windows: int32 [12, 4], replicated, may hold values from 0 to 1
- valid_rows: int32 [8], replicated, may hold values from 1 to 4, as said below
- valid_cols: int32 [8], replicated, may hold values from 1 to 4, as said below
Outputs:
- attended: bfloat16 [4, 32, 32, 1536], P('clip', 'ha', 'wa'), parts along dimension 0
- query_grad: bfloat16 [4, 32, 32, 1536], P('clip', 'ha', 'wa'), parts along dimension 0
- key_grad: bfloat16 [4, 32, 32, 1536], P('clip', 'ha', 'wa'), parts along dimension 0
- value_grad: bfloat16 [4, 32, 32, 1536], P('clip', 'ha', 'wa'), parts along dimension 0
The draws below stay inside these ranges and needn't reach their ends.
There are 2 independent parts, one for each index of `clip`. The reference program is written for one: setup_inputs(seed, part) draws one part's arguments, and reference() takes and returns one part's arrays. A program takes and returns all parts, laid end to end along the dimension named above; an argument that names none is the same for every part. Nothing has to cross between parts.
Inputs may be any that keep to these rules, and one draw needn't show every extreme that they name: `valid_rows`: 4 in the first tile row, 1 in the last. `valid_cols`: 4 in the first tile column, 1 in the last.
All inputs are finite; a program needn't handle non-finite values.
Results may differ from the reference program's by a relative error of at most 0.017.
Values may be sent and summed in bfloat16 or wider, within the bound.
A program may use at most 128 MiB of HBM per device.

```python
import math
import jax
import jax.numpy as jnp
from jax import lax

TILE = 4
FRAMES = 2
HEADS = 12
FEAT = 1536
HT = 32
WT = 32
HTILES = 8
WTILES = 8


def draw_queries(key, part):
    base_draw = 1.2 * jax.random.normal(jax.random.fold_in(key, 1), (FRAMES, HT, WT, FEAT), jnp.float32)
    return jnp.clip(base_draw, -7.0, 7.0).astype(jnp.bfloat16)


def draw_keys(key, part):
    base_draw = 1.2 * jax.random.normal(jax.random.fold_in(key, 2), (FRAMES, HT, WT, FEAT), jnp.float32)
    return jnp.clip(base_draw, -7.0, 7.0).astype(jnp.bfloat16)


def ragged_counts(key, salt, count):
    drawn = jax.random.randint(jax.random.fold_in(key, salt), (count,), 1, TILE + 1)
    positions = jnp.arange(count, dtype=jnp.int32)
    drawn = jnp.where(positions == 0, TILE, drawn)
    return jnp.where(positions == count - 1, 1, drawn).astype(jnp.int32)


def draw_valid_rows(key, part):
    return ragged_counts(key, 31, HTILES)


def draw_valid_cols(key, part):
    return ragged_counts(key, 37, WTILES)


def with_ends(values, stream_key, low, top_value):
    shape = values.shape
    spot = [jax.random.randint(jax.random.fold_in(stream_key, axis), (), 0, shape[axis]) for axis in range(len(shape))]
    values = values.at[tuple(spot)].set(low)
    longest = shape.index(max(shape))
    spot[longest] = (spot[longest] + 1) % shape[longest]
    return values.at[tuple(spot)].set(top_value)


def levels(rng, dims, cuts, least, high):
    def one(axis_at, blocks):
        steps = jax.random.uniform(jax.random.fold_in(jax.random.fold_in(rng, 6), axis_at), (blocks,), jnp.float32, least / len(cuts), high / len(cuts))
        return jnp.repeat(jnp.exp(steps), dims[axis_at] // blocks).reshape((-1,) + (1,) * (len(dims) - axis_at - 1))

    gain = one(*cuts[0])
    for cut in cuts[1:]:
        gain = gain * one(*cut)
    return gain


def normal_values(stream_key, shape, width, limit, shards=(), held_as=jnp.bfloat16):
    loudness = levels(stream_key, shape, shards, -0.22, 0.18) if shards else 1.0
    values = jax.random.normal(stream_key, shape, jnp.float32) * width * loudness
    return jnp.minimum(jnp.maximum(values, -limit), limit).astype(held_as)


def setup_inputs(seed: int = 0, part: int = 0) -> dict:
    key_of = jax.random.split(jax.random.key(seed), 8)
    own_keys = jax.random.split(jax.random.fold_in(key_of[7], part), 8)
    return {
        "queries": draw_queries(jax.random.fold_in(jax.random.fold_in(key_of[7], part), 71), part),
        "keys": draw_keys(jax.random.fold_in(jax.random.fold_in(key_of[7], part), 71), part),
        "values": normal_values(own_keys[2], (FRAMES, HT, WT, FEAT), 3.0, 15.0, ((1, 4), (2, 4))),
        "out_grad": normal_values(own_keys[3], (FRAMES, HT, WT, FEAT), 4.0, 16.0, ((1, 4), (2, 4))),
        "windows": with_ends(jax.random.randint(key_of[4], (HEADS, 4), 0, 2), jax.random.fold_in(key_of[4], 1), 0, 1).astype(jnp.int32),
        "valid_rows": draw_valid_rows(jax.random.fold_in(key_of[7], 71), part),
        "valid_cols": draw_valid_cols(jax.random.fold_in(key_of[7], 71), part),
    }


def span_live(tile_counts, first_cell, cell_total, tile_edge):
    positions = first_cell - tile_edge + jnp.arange(cell_total, dtype=jnp.int32)
    grid_cells = tile_counts.shape[0] * tile_edge
    matches = (positions // tile_edge)[:, None] == jnp.arange(tile_counts.shape[0], dtype=jnp.int32)[None, :]
    row_limit = lax.optimization_barrier(jnp.sum(jnp.where(matches, tile_counts[None, :], 0), axis=1))
    inside = (positions >= 0) & (positions < grid_cells)
    return inside & (positions % tile_edge < row_limit)

def window_table(windows, tile_edge, flipped):
    tile_shift = jnp.arange(3 * tile_edge, dtype=jnp.int32) // tile_edge - 1
    if flipped:
        tile_shift = -tile_shift
    along_rows = (tile_shift[None, :] >= -windows[:, 0:1]) & (tile_shift[None, :] <= windows[:, 1:2])
    along_cols = (tile_shift[None, :] >= -windows[:, 2:3]) & (tile_shift[None, :] <= windows[:, 3:4])
    return (along_rows[:, :, None] & along_cols[:, None, :]).reshape(windows.shape[0], -1)

def mask_rows(window_ok, box_live, frame_count):
    joined = window_ok[None, :, None, :] & box_live[:, None, None, :]
    full_dims = (box_live.shape[0], window_ok.shape[0], frame_count, window_ok.shape[1])
    return jnp.broadcast_to(joined, full_dims).reshape(full_dims[0], full_dims[1], -1)

def box_tiles(padded_block, tile_edge, tiles_down, tiles_across):
    box_list = [padded_block[:, row_tile * tile_edge:(row_tile + 3) * tile_edge, col_tile * tile_edge:(col_tile + 3) * tile_edge] for row_tile in range(tiles_down) for col_tile in range(tiles_across)]
    stacked = jnp.stack(box_list)
    return stacked.reshape(stacked.shape[0], -1, stacked.shape[-1])

def center_tiles(block_data, tile_edge):
    frame_count, block_rows, block_cols, channels = block_data.shape
    split_cells = block_data.reshape(frame_count, block_rows // tile_edge, tile_edge, block_cols // tile_edge, tile_edge, channels)
    return split_cells.transpose(1, 3, 0, 2, 4, 5).reshape(-1, frame_count * tile_edge * tile_edge, channels)

def tiles_grid(tile_data, frame_count, tiles_down, tiles_across, tile_edge):
    channels = tile_data.shape[-1]
    split_cells = tile_data.reshape(tiles_down, tiles_across, frame_count, tile_edge, tile_edge, channels)
    return split_cells.transpose(2, 0, 3, 1, 4, 5).reshape(frame_count, tiles_down * tile_edge, tiles_across * tile_edge, channels)

def rounded(array):
    return lax.optimization_barrier(array.astype(jnp.bfloat16)).astype(jnp.float32)

def reference(queries, keys, values, out_grad, windows, valid_rows, valid_cols):
    tile_edge = TILE
    frame_count, grid_rows, grid_cols, features = queries.shape
    head_count = windows.shape[0]
    head_size = features // head_count
    score_scale = 1.0 / math.sqrt(head_size)
    tiles_down = grid_rows // tile_edge
    tiles_across = grid_cols // tile_edge
    live_pad = span_live(valid_rows, 0, grid_rows + 2 * tile_edge, tile_edge)[:, None] & span_live(valid_cols, 0, grid_cols + 2 * tile_edge, tile_edge)[None, :]
    live_source = live_pad[None, :, :, None]
    live_grid = live_pad[None, tile_edge:-tile_edge, tile_edge:-tile_edge, None]
    pad_spec = ((0, 0), (tile_edge, tile_edge), (tile_edge, tile_edge), (0, 0))
    keys_pad = jnp.pad(keys, pad_spec)
    values_pad = jnp.pad(values, pad_spec)
    queries_pad = jnp.pad(queries, pad_spec)
    grad_pad = jnp.pad(out_grad, pad_spec)
    forward_ok = window_table(windows, tile_edge, False)
    backward_ok = window_table(windows, tile_edge, True)

    def band_boxes(padded, row_tile):
        band_rows = lax.dynamic_slice_in_dim(padded, (row_tile * tile_edge).astype(jnp.int32), 3 * tile_edge, axis=1)
        return box_tiles(band_rows, tile_edge, 1, tiles_across)

    def band_centers(array, row_tile):
        band_rows = lax.dynamic_slice_in_dim(array, (row_tile * tile_edge).astype(jnp.int32), tile_edge, axis=1)
        return center_tiles(band_rows, tile_edge)

    def heads_of(tile_data):
        return tile_data.reshape(tile_data.shape[0], tile_data.shape[1], head_count, head_size).astype(jnp.float32)

    def query_live(row_tile):
        cell_flags = band_centers(live_grid, row_tile)[:, :, 0]
        return jnp.broadcast_to(cell_flags[:, None, :], (tiles_across, frame_count, cell_flags.shape[1])).reshape(tiles_across, -1)

    def forward_parts(row_tile):
        query_tiles = heads_of(band_centers(queries, row_tile))
        key_boxes = heads_of(band_boxes(keys_pad, row_tile))
        value_boxes = heads_of(band_boxes(values_pad, row_tile))
        allowed = mask_rows(forward_ok, band_boxes(live_source, row_tile)[:, :, 0], frame_count)
        query_ok = query_live(row_tile).astype(jnp.float32)
        scores = jnp.einsum('bqhd,bkhd->bhqk', query_tiles, key_boxes) * score_scale
        masked = jnp.where(allowed[:, :, None, :], scores, -jnp.inf)
        return (key_boxes, value_boxes, masked, query_ok)

    def forward_row(row_tile):
        key_boxes, value_boxes, masked, query_ok = forward_parts(row_tile)
        top_score = lax.optimization_barrier(jnp.max(masked, axis=-1, keepdims=True))
        log_total = top_score[..., 0] + jnp.log(lax.optimization_barrier(jnp.sum(jnp.exp(masked - top_score), axis=-1)))
        weights = jnp.exp(masked - log_total[..., None]) * query_ok[:, None, :, None]
        output = jnp.einsum('bhqk,bkhd->bqhd', rounded(weights), value_boxes).astype(jnp.bfloat16)
        return (output.reshape(tiles_across, -1, features), log_total.transpose(0, 2, 1))

    def to_grid(stacked):
        merged = stacked.reshape(tiles_down * tiles_across, stacked.shape[2], stacked.shape[3])
        return tiles_grid(merged, frame_count, tiles_down, tiles_across, tile_edge)
    rows_index = jnp.arange(tiles_down, dtype=jnp.int32)
    attended_rows, log_rows = lax.map(forward_row, rows_index)
    attended = to_grid(attended_rows)
    log_totals = to_grid(log_rows)
    products = (attended.astype(jnp.float32) * out_grad.astype(jnp.float32)).reshape(frame_count, grid_rows, grid_cols, head_count, head_size)
    grad_dots = lax.optimization_barrier(jnp.sum(products, axis=-1))

    def query_row(row_tile):
        key_boxes, value_boxes, masked, query_ok = forward_parts(row_tile)
        grad_tiles = heads_of(band_centers(out_grad, row_tile))
        log_total = band_centers(log_totals, row_tile).transpose(0, 2, 1)
        dots_here = band_centers(grad_dots, row_tile).transpose(0, 2, 1)
        weights = jnp.exp(masked - log_total[..., None]) * query_ok[:, None, :, None]
        prob_grad = jnp.einsum('bqhd,bkhd->bhqk', grad_tiles, value_boxes)
        score_grad = rounded(weights * (prob_grad - dots_here[..., None]))
        result = (jnp.einsum('bhqk,bkhd->bqhd', score_grad, key_boxes) * score_scale).astype(jnp.bfloat16)
        return result.reshape(tiles_across, -1, features)
    query_grad = to_grid(lax.map(query_row, rows_index))
    log_pad = jnp.pad(log_totals, pad_spec)
    dots_pad = jnp.pad(grad_dots, pad_spec)

    def key_row(row_tile):
        query_boxes = heads_of(band_boxes(queries_pad, row_tile))
        grad_boxes = heads_of(band_boxes(grad_pad, row_tile))
        log_boxes = band_boxes(log_pad, row_tile).transpose(0, 2, 1)
        dots_boxes = band_boxes(dots_pad, row_tile).transpose(0, 2, 1)
        key_tiles = heads_of(band_centers(keys, row_tile))
        value_tiles = heads_of(band_centers(values, row_tile))
        allowed = mask_rows(backward_ok, band_boxes(live_source, row_tile)[:, :, 0], frame_count)
        joined = allowed[:, :, :, None] & query_live(row_tile)[:, None, None, :]
        scores = jnp.einsum('bqhd,bkhd->bhqk', query_boxes, key_tiles) * score_scale
        weights = jnp.where(joined, jnp.exp(scores - log_boxes[..., None]), 0.0)
        value_part = jnp.einsum('bhqk,bqhd->bkhd', rounded(weights), grad_boxes).astype(jnp.bfloat16)
        prob_grad = jnp.einsum('bqhd,bkhd->bhqk', grad_boxes, value_tiles)
        score_grad = rounded(weights * (prob_grad - dots_boxes[..., None]))
        key_part = (jnp.einsum('bhqk,bqhd->bkhd', score_grad, query_boxes) * score_scale).astype(jnp.bfloat16)
        return (key_part.reshape(tiles_across, -1, features), value_part.reshape(tiles_across, -1, features))
    key_rows, value_rows = lax.map(key_row, rows_index)
    return (attended, query_grad, to_grid(key_rows), to_grid(value_rows))
```

```python
import functools
import math

import jax
import jax.numpy as jnp
from jax import lax
from jax.experimental import pallas as pl
from jax.experimental.pallas import tpu as pltpu
from jax.sharding import PartitionSpec as P

TILE = 4
SIZES = (2,) * 6
NEG = -1e30
MESH = pl.DeviceIdType.MESH
F32 = jnp.float32
BF16 = jnp.bfloat16

KINDS = 12
Z_S, Z_N, W_E, W_W, C_E, C_W, GC_E, GC_W, GO_E, GO_W, GH_S, GH_N = range(KINDS)
EARLY = 3
AHEAD = 2
BEHIND = 2
OWN = 2
ORDER = (1, 2, 0, 3)


def split(heads):
    edges = [0]
    for size in SIZES:
        edges.append(min(edges[-1] + size, heads))
    edges += range(edges[-1] + 1, heads + 1)
    return [(a, b) for a, b in zip(edges, edges[1:]) if b > a]


def iota(shape, dim):
    return lax.broadcasted_iota(jnp.int32, shape, dim)


def native_of(a):
    tr, tc, f, r, c = a >> 6, (a >> 5) & 1, (a >> 4) & 1, (a >> 2) & 3, a & 3
    return f * 64 + (tr * 4 + r) * 8 + tc * 4 + c


def dot(a, b, dims):
    return lax.dot_general(a, b, (dims, ((), ())), preferred_element_type=F32)


NT = ((1,), (1,))
NN = ((1,), (0,))
TN = ((0,), (0,))


def kernel(
    heads, n_ha, n_wa,
    q_hbm, k_hbm, v_hbm, g_hbm, win_hbm, vr_hbm, vc_hbm,
    att_ref, dq_ref, dk_ref, dv_ref,
    q_ref, k_ref, v_ref, g_ref, win_ref, vr_ref, vc_ref, kv, gw, gwr, gh, ghr, acc, kb, load, send, recv,
):
    size = kv.shape[-1]
    parts = split(heads)
    chunks = len(parts)
    scale = 1.0 / math.sqrt(size)
    ha, wa = lax.axis_index("ha"), lax.axis_index("wa")
    has_n, has_s = ha > 0, ha < n_ha - 1
    has_w, has_e = wa > 0, wa < n_wa - 1
    to_n, to_s = {"ha": ha - 1}, {"ha": ha + 1}
    to_w, to_e = {"wa": wa - 1}, {"wa": wa + 1}

    loads = [
        pltpu.make_async_copy(src, dst, load.at[i])
        for i, (src, dst) in enumerate(
            (
                (k_hbm, k_ref), (v_hbm, v_ref), (q_hbm, q_ref), (g_hbm, g_ref),
                (win_hbm, win_ref), (vr_hbm, vr_ref), (vc_hbm, vc_ref),
            )
        )
    ]
    for copy in loads:
        copy.start()

    barrier = pltpu.get_barrier_semaphore()
    expected = 0
    for has, to in ((has_n, to_n), (has_s, to_s), (has_w, to_w), (has_e, to_e)):
        expected = expected + has.astype(jnp.int32)

        @pl.when(has)
        def _():
            pl.semaphore_signal(barrier, inc=1, device_id=to, device_id_type=MESH)

    cells = 128
    perm = jnp.where(native_of(iota((cells, cells), 0)) == iota((cells, cells), 1), 1.0, 0.0)
    perm = perm.astype(BF16)
    back = jnp.where(native_of(iota((cells, cells), 1)) == iota((cells, cells), 0), 1.0, 0.0)
    back = back.astype(BF16)

    def flat(ref, lo, width):
        return ref[:, :, :, lo : lo + width].astype(F32).reshape(cells, width).astype(BF16)

    def permute(c):
        first, last = parts[c]
        for t, ref in enumerate((k_ref, v_ref)):
            width = (last - first) * size
            tiles = dot(perm, flat(ref, first * size, width), NN).astype(BF16)
            for h in range(first, last):
                lo = (h - first) * size
                kv[h, t, 0:2, 1:3] = tiles[:, lo : lo + size].reshape(2, 2, 32, size)

    def message(kind, c, src, dst, to):
        return pltpu.make_async_remote_copy(
            src_ref=src, dst_ref=dst, send_sem=send.at[kind], recv_sem=recv.at[kind, c],
            device_id=to, device_id_type=MESH,
        )

    def build(kind, c, part):
        at = slice(*part)
        if kind == Z_S:
            return message(kind, c, kv.at[at, :, 1, 1:3], kv.at[at, :, 2, 1:3], to_s), has_s, has_n
        if kind == Z_N:
            return message(kind, c, kv.at[at, :, 0, 1:3], kv.at[at, :, 3, 1:3], to_n), has_n, has_s
        if kind in (W_E, W_W, C_E, C_W):
            span = slice(0, 2) if kind in (W_E, W_W) else slice(2, 4)
            if kind in (W_E, C_E):
                copy = message(kind, c, kv.at[at, :, span, 2], kv.at[at, :, span, 0], to_e)
                return copy, has_e, has_w
            copy = message(kind, c, kv.at[at, :, span, 1], kv.at[at, :, span, 3], to_w)
            return copy, has_w, has_e
        if kind in (GC_E, GC_W, GO_E, GO_W):
            span = slice(2, 4) if kind in (GC_E, GC_W) else slice(0, 2)
            if kind in (GC_E, GO_E):
                copy = message(kind, c, gw.at[at, 1, :, span], gwr.at[at, 0, :, span], to_e)
                return copy, has_e, has_w
            copy = message(kind, c, gw.at[at, 0, :, span], gwr.at[at, 1, :, span], to_w)
            return copy, has_w, has_e
        if kind == GH_S:
            return message(kind, c, gh.at[at, 1], ghr.at[at, 0], to_s), has_s, has_n
        return message(kind, c, gh.at[at, 0], ghr.at[at, 1], to_n), has_n, has_s

    def start(c, *kinds):
        for kind in kinds:
            copy, sends, _ = build(kind, c, parts[c])
            pl.when(sends)(copy.start)

    def arrive(c, *kinds):
        for kind in kinds:
            copy, _, gets = build(kind, c, parts[c])
            pl.when(gets)(copy.wait_recv)

    loads[0].wait()
    loads[1].wait()
    permute(0)
    for c in range(chunks):
        if c + 1 < chunks:
            permute(c + 1)
        if c == 0:
            pl.semaphore_wait(barrier, expected)
        start(c, Z_S, Z_N)
        if c < EARLY:
            start(c, W_E, W_W)

    def clear(has, ref, *index):
        @pl.when(jnp.logical_not(has))
        def _():
            view = ref.at[index]
            view[...] = jnp.zeros(view.shape, ref.dtype)

    every = slice(None)
    clear(has_n, kv, every, every, 2, slice(1, 3))
    clear(has_s, kv, every, every, 3, slice(1, 3))
    clear(has_w, kv, every, every, every, 0)
    clear(has_e, kv, every, every, every, 3)
    clear(has_w, gwr, every, 0)
    clear(has_e, gwr, every, 1)
    clear(has_n, ghr, every, 0)
    clear(has_s, ghr, every, 1)

    for copy in loads[4:]:
        copy.wait()

    def limits(ref, first):
        count = ref.shape[0]
        out = []
        for e in range(4):
            at = first + e
            inside = (at >= 0) & (at < count)
            out.append(jnp.where(inside, ref[jnp.clip(at, 0, count - 1)], 0))
        return out

    rows, cols = limits(vr_ref, ha * 2 - 1), limits(vc_ref, wa * 2 - 1)
    lane = iota((1, cells), 1)
    lane_r, lane_c = (lane >> 3) & 7, lane & 7
    tile_r, tile_c = (lane_r >> 2) + 1, (lane_c >> 2) + 1
    live = ((lane_r & 3) < jnp.where(tile_r == 1, rows[1], rows[2])) & (
        (lane_c & 3) < jnp.where(tile_c == 1, cols[1], cols[2])
    )
    live = jnp.where(live, 1.0, 0.0).astype(F32)
    sub = iota((32, cells), 0)
    for er in range(4):
        for ec in range(4):
            ok = (((sub >> 2) & 3) < rows[ORDER[er]]) & ((sub & 3) < cols[ec])
            kb[er * 4 + ec] = jnp.where(ok, 0.0, NEG)

    def attend(h):
        lo = h * size
        w = [win_ref[j, h] for j in range(4)]
        row_bias = [
            jnp.where((e - tile_r >= -w[0]) & (e - tile_r <= w[1]), 0.0, NEG) for e in range(4)
        ]
        col_bias = [
            jnp.where((e - tile_c >= -w[2]) & (e - tile_c <= w[3]), 0.0, NEG) for e in range(4)
        ]
        q = flat(q_ref, lo, size)
        g = flat(g_ref, lo, size)
        key = kv[h, 0].reshape(512, size)
        val = kv[h, 1].reshape(512, size)
        raw = dot(key, q, NT)
        s = [
            raw[t * 32 : t * 32 + 32] * scale + (kb[t] + (row_bias[ORDER[t // 4]] + col_bias[t % 4]))
            for t in range(16)
        ]
        top = jnp.max(functools.reduce(jnp.maximum, s), axis=0, keepdims=True)
        e = [jnp.exp(x - top) for x in s]
        total = jnp.sum(sum(e[1:], e[0]), axis=0, keepdims=True)
        inv = live / total
        p = [x * inv for x in e]
        low = [x.astype(BF16) for x in p]
        low_all = jnp.concatenate(low, axis=0)
        out = dot(low_all, val, TN)
        att_ref[:, :, :, lo : lo + size] = out.reshape(2, 8, 8, size).astype(BF16)
        raw_d = dot(val, g, NT)
        dp = [raw_d[t * 32 : t * 32 + 32] for t in range(16)]
        prod = [a.astype(F32) * b for a, b in zip(low, dp)]
        dots = jnp.sum(sum(prod[1:], prod[0]), axis=0, keepdims=True)
        ds = jnp.concatenate([(a * (b - dots)).astype(BF16) for a, b in zip(p, dp)], axis=0)
        dq = dot(ds, key, TN) * scale
        dq_ref[:, :, :, lo : lo + size] = dq.reshape(2, 8, 8, size).astype(BF16)
        dk = dot(ds, q, NN) * scale
        dv = dot(low_all, g, NN)
        for t, part in enumerate((dk, dv)):
            part = part.reshape(4, 4, 32, size)
            for side, col in ((0, 0), (1, 3)):
                gw[h, side, t] = part[:, col].astype(BF16)
            acc[h, t] = part[:, 1:3]

    def fold_width(c):
        arrive(c, GC_E, GC_W)
        for h in range(*parts[c]):
            for t in range(2):
                for side in range(2):
                    both = acc[h, t, 2:4, side] + gwr[h, side, t, 2:4].astype(F32)
                    gh[h, 0, t, side] = both[0].astype(BF16)
                    gh[h, 1, t, side] = both[1].astype(BF16)
        start(c, GH_S, GH_N)

    def fold_height(c):
        arrive(c, GO_E, GO_W, GH_S, GH_N)
        for h in range(*parts[c]):
            for t, ref in enumerate((dk_ref, dv_ref)):
                total = acc[h, t, 0:2] + ghr[h, :, t].astype(F32)
                got = [gwr[h, side, t, 0:2].astype(F32) for side in range(2)]
                total = total + jnp.stack(got, axis=1)
                tiles = total.reshape(cells, size).astype(BF16)
                grid = dot(back, tiles, NN)
                ref[:, :, :, h * size : (h + 1) * size] = grid.reshape(2, 8, 8, size).astype(BF16)

    def forward(c):
        arrive(c, Z_S, Z_N)
        start(c, C_E, C_W)
        if c + EARLY < chunks:
            start(c + EARLY, W_E, W_W)

    sent = 0
    for c in range(min(AHEAD, chunks)):
        forward(c)
    loads[2].wait()
    loads[3].wait()
    for step in range(chunks):
        if step + AHEAD < chunks:
            forward(step + AHEAD)
        arrive(step, W_E, W_W, C_E, C_W)
        for h in range(*parts[step]):
            attend(h)
        start(step, GC_E, GC_W)
        if step >= BEHIND:
            fold_width(step - BEHIND)
        if step + AHEAD >= chunks:
            for c in range(sent, min(step, sent + OWN)):
                start(c, GO_E, GO_W)
                sent = c + 1
    for c in range(max(chunks - BEHIND, 0), chunks):
        for i in range(sent, min(chunks, sent + OWN)):
            start(i, GO_E, GO_W)
            sent = i + 1
        fold_width(c)
    for c in range(sent, chunks):
        start(c, GO_E, GO_W)
    for c in range(chunks):
        fold_height(c)

    for kind in range(KINDS):
        copy, sends, _ = build(kind, 0, (0, heads))
        pl.when(sends)(copy.wait_send)


def store(*refs):
    sem = refs[-1]
    count = len(refs) // 2
    copies = [
        pltpu.make_async_copy(refs[i], refs[count + i], sem.at[i]) for i in range(count)
    ]
    for copy in copies:
        copy.start()
    for copy in copies:
        copy.wait()


def local(n_ha, n_wa, queries, keys, values, out_grad, windows, valid_rows, valid_cols):
    heads = windows.shape[0]
    size = queries.shape[-1] // heads
    vmem = pl.BlockSpec(memory_space=pltpu.VMEM)
    hbm = pl.BlockSpec(memory_space=pltpu.HBM)
    shape = jax.ShapeDtypeStruct(queries.shape, BF16)
    held = [
        pltpu.with_memory_space_constraint(x, pltpu.HBM)
        for x in (queries, keys, values, out_grad, windows.T, valid_rows, valid_cols)
    ]
    results = pl.pallas_call(
        functools.partial(kernel, heads, n_ha, n_wa),
        out_shape=(shape,) * 4,
        in_specs=[hbm] * 7,
        out_specs=(vmem,) * 4,
        scratch_shapes=[pltpu.VMEM(queries.shape, BF16)] * 4
        + [
            pltpu.SMEM((4, heads), jnp.int32),
            pltpu.SMEM(valid_rows.shape, jnp.int32),
            pltpu.SMEM(valid_cols.shape, jnp.int32),
            pltpu.VMEM((heads, 2, 4, 4, 32, size), BF16),
            pltpu.VMEM((heads, 2, 2, 4, 32, size), BF16),
            pltpu.VMEM((heads, 2, 2, 4, 32, size), BF16),
            pltpu.VMEM((heads, 2, 2, 2, 32, size), BF16),
            pltpu.VMEM((heads, 2, 2, 2, 32, size), BF16),
            pltpu.VMEM((heads, 2, 4, 2, 32, size), F32),
            pltpu.VMEM((16, 32, 128), F32),
            pltpu.SemaphoreType.DMA((7,)),
            pltpu.SemaphoreType.DMA((KINDS,)),
            pltpu.SemaphoreType.DMA((KINDS, len(split(heads)))),
        ],
        compiler_params=pltpu.CompilerParams(
            collective_id=0, has_side_effects=True, vmem_limit_bytes=40 << 20
        ),
    )(*held)
    return pl.pallas_call(
        store,
        out_shape=(shape,) * 4,
        in_specs=[pl.BlockSpec(memory_space=pl.ANY)] * 4,
        out_specs=(hbm,) * 4,
        scratch_shapes=[pltpu.SemaphoreType.DMA((4,))],
        compiler_params=pltpu.CompilerParams(vmem_limit_bytes=1 << 20),
    )(*results)


def solution(mesh):
    cells = P("clip", "ha", "wa", None)
    body = functools.partial(local, mesh.shape["ha"], mesh.shape["wa"])
    return jax.shard_map(
        body,
        mesh=mesh,
        in_specs=(cells,) * 4 + (P(),) * 3,
        out_specs=(cells,) * 4,
        check_vma=False,
    )
```

```python
import functools
import math

import jax
import jax.numpy as jnp
from jax import lax
from jax.experimental import pallas as pl
from jax.experimental.pallas import tpu as pltpu
from jax.sharding import PartitionSpec as P

TILE = 4
SIZES = (1,) * 12
NEG = -1e30
MESH = pl.DeviceIdType.MESH
F32 = jnp.float32
BF16 = jnp.bfloat16

KINDS = 12
Z_S, Z_N, W_E, W_W, C_E, C_W, GC_E, GC_W, GO_E, GO_W, GH_S, GH_N = range(KINDS)
EARLY = 9
AHEAD = 4
BEHIND = 4
LATE = 6
WIDE = (1,) * 12
OWNS = (1,) * 12
TILES = (
    (1, 1), (1, 2), (2, 1), (2, 2), (0, 1), (0, 2), (3, 1), (3, 2),
    (1, 0), (2, 0), (0, 0), (3, 0), (1, 3), (2, 3), (0, 3), (3, 3),
)


def split(heads, sizes):
    edges = [0]
    for size in sizes:
        edges.append(min(edges[-1] + size, heads))
    edges += range(edges[-1] + 1, heads + 1)
    return [(a, b) for a, b in zip(edges, edges[1:]) if b > a]


def iota(shape, dim):
    return lax.broadcasted_iota(jnp.int32, shape, dim)


def native_of(a):
    tr, tc, f, r, c = a >> 6, (a >> 5) & 1, (a >> 4) & 1, (a >> 2) & 3, a & 3
    return f * 64 + (tr * 4 + r) * 8 + tc * 4 + c


def dot(a, b, dims):
    return lax.dot_general(a, b, (dims, ((), ())), preferred_element_type=F32)


NT = ((1,), (1,))
NN = ((1,), (0,))
TN = ((0,), (0,))


def kernel(
    heads, n_ha, n_wa,
    q_hbm, k_hbm, v_hbm, g_hbm, win_hbm, vr_hbm, vc_hbm,
    att_ref, dq_ref, dk_ref, dv_ref,
    q_ref, k_ref, v_ref, g_ref, win_ref, vr_ref, vc_ref, own, zin, win, gw, gwr, gh, ghr, acc, kb, load, send, recv,
):
    size = own.shape[-1]
    parts = split(heads, SIZES)
    chunks = len(parts)
    scale = 1.0 / math.sqrt(size)
    ha, wa = lax.axis_index("ha"), lax.axis_index("wa")
    has_n, has_s = ha > 0, ha < n_ha - 1
    has_w, has_e = wa > 0, wa < n_wa - 1
    to_n, to_s = {"ha": ha - 1}, {"ha": ha + 1}
    to_w, to_e = {"wa": wa - 1}, {"wa": wa + 1}

    loads = [
        pltpu.make_async_copy(src, dst, load.at[i])
        for i, (src, dst) in enumerate(
            (
                (k_hbm, k_ref), (v_hbm, v_ref), (q_hbm, q_ref), (g_hbm, g_ref),
                (win_hbm, win_ref), (vr_hbm, vr_ref), (vc_hbm, vc_ref),
            )
        )
    ]
    for copy in loads:
        copy.start()

    barrier = pltpu.get_barrier_semaphore()
    expected = 0
    for has, to in ((has_n, to_n), (has_s, to_s), (has_w, to_w), (has_e, to_e)):
        expected = expected + has.astype(jnp.int32)

        @pl.when(has)
        def _():
            pl.semaphore_signal(barrier, inc=1, device_id=to, device_id_type=MESH)

    cells = 128
    perm = jnp.where(native_of(iota((cells, cells), 0)) == iota((cells, cells), 1), 1.0, 0.0)
    perm = perm.astype(BF16)
    back = jnp.where(native_of(iota((cells, cells), 1)) == iota((cells, cells), 0), 1.0, 0.0)
    back = back.astype(BF16)

    def flat(ref, lo, width):
        return ref[:, :, :, lo : lo + width].astype(F32).reshape(cells, width).astype(BF16)

    def permute(c):
        first, last = parts[c]
        for t, ref in enumerate((k_ref, v_ref)):
            width = (last - first) * size
            tiles = dot(perm, flat(ref, first * size, width), NN).astype(BF16)
            for h in range(first, last):
                lo = (h - first) * size
                own[h, :, t] = tiles[:, lo : lo + size].reshape(2, 2, 32, size)

    routes = {
        "n": (to_n, has_n, has_s), "s": (to_s, has_s, has_n),
        "w": (to_w, has_w, has_e), "e": (to_e, has_e, has_w),
    }
    half = {GO_E: slice(0, 2), GO_W: slice(0, 2), GC_E: slice(2, 4), GC_W: slice(2, 4)}

    def ends(kind, at):
        if kind == Z_S:
            return "s", own.at[at, 1], zin.at[at, 0]
        if kind == Z_N:
            return "n", own.at[at, 0], zin.at[at, 1]
        if kind == W_E:
            return "e", own.at[at, :, :, 1], win.at[0, at, 0:2]
        if kind == W_W:
            return "w", own.at[at, :, :, 0], win.at[1, at, 0:2]
        if kind == C_E:
            return "e", zin.at[at, :, :, 1], win.at[0, at, 2:4]
        if kind == C_W:
            return "w", zin.at[at, :, :, 0], win.at[1, at, 2:4]
        if kind in (GC_E, GO_E):
            return "e", gw.at[1, at, half[kind]], gwr.at[0, at, half[kind]]
        if kind in (GC_W, GO_W):
            return "w", gw.at[0, at, half[kind]], gwr.at[1, at, half[kind]]
        if kind == GH_S:
            return "s", gh.at[1, at], ghr.at[0, at]
        return "n", gh.at[0, at], ghr.at[1, at]

    def build(kind, c, part):
        way, src, dst = ends(kind, slice(*part))
        to, sends, gets = routes[way]
        copy = pltpu.make_async_remote_copy(
            src_ref=src, dst_ref=dst, send_sem=send.at[kind], recv_sem=recv.at[kind, c],
            device_id=to, device_id_type=MESH,
        )
        return copy, sends, gets

    cuts = {kind: parts for kind in range(KINDS)}
    cuts[W_E] = cuts[W_W] = split(heads, WIDE)
    cuts[GO_E] = cuts[GO_W] = split(heads, OWNS)
    begun, ended = [0] * KINDS, [0] * KINDS

    def begin(last, *kinds):
        for kind in kinds:
            while begun[kind] < len(cuts[kind]) and cuts[kind][begun[kind]][1] <= last:
                copy, sends, _ = build(kind, begun[kind], cuts[kind][begun[kind]])
                pl.when(sends)(copy.start)
                begun[kind] += 1

    def arrive(last, *kinds):
        for kind in kinds:
            while ended[kind] < len(cuts[kind]) and cuts[kind][ended[kind]][0] < last:
                copy, _, gets = build(kind, ended[kind], cuts[kind][ended[kind]])
                pl.when(gets)(copy.wait_recv)
                ended[kind] += 1

    loads[0].wait()
    loads[1].wait()
    permute(0)
    for c in range(chunks):
        if c + 1 < chunks:
            permute(c + 1)
        if c == 0:
            pl.semaphore_wait(barrier, expected)
        begin(parts[c][1], Z_S, Z_N)
        begin(min(parts[c][1], EARLY), W_E, W_W)

    def clear(has, ref, *index):
        @pl.when(jnp.logical_not(has))
        def _():
            view = ref.at[index]
            view[...] = jnp.zeros(view.shape, ref.dtype)

    every = slice(None)
    clear(has_n, zin, every, 0)
    clear(has_s, zin, every, 1)
    clear(has_w, win, 0)
    clear(has_e, win, 1)
    clear(has_w, gwr, 0)
    clear(has_e, gwr, 1)
    clear(has_n, ghr, 0)
    clear(has_s, ghr, 1)

    for copy in loads[4:]:
        copy.wait()

    def limits(ref, first):
        count = ref.shape[0]
        out = []
        for e in range(4):
            at = first + e
            inside = (at >= 0) & (at < count)
            out.append(jnp.where(inside, ref[jnp.clip(at, 0, count - 1)], 0))
        return out

    rows, cols = limits(vr_ref, ha * 2 - 1), limits(vc_ref, wa * 2 - 1)
    lane = iota((1, cells), 1)
    lane_r, lane_c = (lane >> 3) & 7, lane & 7
    tile_r, tile_c = (lane_r >> 2) + 1, (lane_c >> 2) + 1
    live = ((lane_r & 3) < jnp.where(tile_r == 1, rows[1], rows[2])) & (
        (lane_c & 3) < jnp.where(tile_c == 1, cols[1], cols[2])
    )
    live = jnp.where(live, 1.0, 0.0).astype(F32)
    sub = iota((32, cells), 0)
    for t, (er, ec) in enumerate(TILES):
        ok = (((sub >> 2) & 3) < rows[er]) & ((sub & 3) < cols[ec])
        kb[t] = jnp.where(ok, 0.0, NEG)

    def attend(h):
        lo = h * size
        w = [win_ref[j, h] for j in range(4)]
        row_bias = [
            jnp.where((e - tile_r >= -w[0]) & (e - tile_r <= w[1]), 0.0, NEG) for e in range(4)
        ]
        col_bias = [
            jnp.where((e - tile_c >= -w[2]) & (e - tile_c <= w[3]), 0.0, NEG) for e in range(4)
        ]
        q = flat(q_ref, lo, size)
        g = flat(g_ref, lo, size)
        key, val = (
            jnp.concatenate(
                [
                    own[h, :, t].reshape(128, size), zin[h, :, t].reshape(128, size),
                    win[0, h, :, t].reshape(128, size), win[1, h, :, t].reshape(128, size),
                ],
                axis=0,
            )
            for t in range(2)
        )
        raw = dot(key, q, NT)
        s = [
            raw[t * 32 : t * 32 + 32] * scale + (kb[t] + (row_bias[er] + col_bias[ec]))
            for t, (er, ec) in enumerate(TILES)
        ]
        top = jnp.max(functools.reduce(jnp.maximum, s), axis=0, keepdims=True)
        e = [jnp.exp(x - top) for x in s]
        total = jnp.sum(sum(e[1:], e[0]), axis=0, keepdims=True)
        inv = live / total
        p = [x * inv for x in e]
        low = [x.astype(BF16) for x in p]
        low_all = jnp.concatenate(low, axis=0)
        out = dot(low_all, val, TN)
        att_ref[:, :, :, lo : lo + size] = out.reshape(2, 8, 8, size).astype(BF16)
        raw_d = dot(val, g, NT)
        dp = [raw_d[t * 32 : t * 32 + 32] for t in range(16)]
        prod = [a.astype(F32) * b for a, b in zip(low, dp)]
        dots = jnp.sum(sum(prod[1:], prod[0]), axis=0, keepdims=True)
        ds = jnp.concatenate([(a * (b - dots)).astype(BF16) for a, b in zip(p, dp)], axis=0)
        dq = dot(ds, key, TN) * scale
        dq_ref[:, :, :, lo : lo + size] = dq.reshape(2, 8, 8, size).astype(BF16)
        dk = dot(ds, q, NN) * scale
        dv = dot(low_all, g, NN)
        for t, part in enumerate((dk, dv)):
            acc[h, t] = part[0:256].reshape(8, 32, size)
            for side in range(2):
                rim = part[256 + side * 128 : 384 + side * 128]
                gw[side, h, :, t] = rim.reshape(4, 32, size).astype(BF16)

    def fold_width(c):
        arrive(parts[c][1], GC_E, GC_W)
        for h in range(*parts[c]):
            for t in range(2):
                for ns in range(2):
                    for col in range(2):
                        both = acc[h, t, 4 + ns * 2 + col] + gwr[col, h, 2 + ns, t].astype(F32)
                        gh[ns, h, t, col] = both.astype(BF16)
        begin(parts[c][1], GH_S, GH_N)

    def fold_height(c):
        arrive(parts[c][1], GO_E, GO_W, GH_S, GH_N)
        for t, ref in enumerate((dk_ref, dv_ref)):
            both = []
            for h in range(*parts[c]):
                tiles = [
                    acc[h, t, r * 2 + col] + ghr[r, h, t, col].astype(F32) + gwr[col, h, r, t].astype(F32)
                    for r in range(2)
                    for col in range(2)
                ]
                both.append(jnp.concatenate(tiles, axis=0).astype(BF16))
            lo, width = parts[c][0] * size, len(both) * size
            grid = dot(back, jnp.concatenate(both, axis=1), NN)
            ref[:, :, :, lo : lo + width] = grid.reshape(2, 8, 8, width).astype(BF16)

    def forward(c):
        arrive(parts[c][1], Z_S, Z_N)
        begin(parts[c][1], C_E, C_W)
        begin(parts[c][1] + EARLY, W_E, W_W)

    for c in range(min(AHEAD, chunks)):
        forward(c)
    loads[2].wait()
    loads[3].wait()
    for step in range(chunks):
        if step + AHEAD < chunks:
            forward(step + AHEAD)
        arrive(parts[step][1], W_E, W_W, C_E, C_W)
        for h in range(*parts[step]):
            attend(h)
        begin(parts[step][1], GC_E, GC_W)
        if step >= BEHIND:
            fold_width(step - BEHIND)
        begin(parts[step][1] - LATE, GO_E, GO_W)
    for c in range(max(chunks - BEHIND, 0), chunks):
        fold_width(c)
        begin(parts[c][1], GO_E, GO_W)
    for c in range(chunks):
        fold_height(c)

    for kind in range(KINDS):
        copy, sends, _ = build(kind, 0, (0, heads))
        pl.when(sends)(copy.wait_send)


def store(*refs):
    sem = refs[-1]
    count = len(refs) // 2
    copies = [
        pltpu.make_async_copy(refs[i], refs[count + i], sem.at[i]) for i in range(count)
    ]
    for copy in copies:
        copy.start()
    for copy in copies:
        copy.wait()


def local(n_ha, n_wa, queries, keys, values, out_grad, windows, valid_rows, valid_cols):
    heads = windows.shape[0]
    size = queries.shape[-1] // heads
    vmem = pl.BlockSpec(memory_space=pltpu.VMEM)
    hbm = pl.BlockSpec(memory_space=pltpu.HBM)
    shape = jax.ShapeDtypeStruct(queries.shape, BF16)
    held = [
        pltpu.with_memory_space_constraint(x, pltpu.HBM)
        for x in (queries, keys, values, out_grad, windows.T, valid_rows, valid_cols)
    ]
    results = pl.pallas_call(
        functools.partial(kernel, heads, n_ha, n_wa),
        out_shape=(shape,) * 4,
        in_specs=[hbm] * 7,
        out_specs=(vmem,) * 4,
        scratch_shapes=[pltpu.VMEM(queries.shape, BF16)] * 4
        + [
            pltpu.SMEM((4, heads), jnp.int32),
            pltpu.SMEM(valid_rows.shape, jnp.int32),
            pltpu.SMEM(valid_cols.shape, jnp.int32),
            pltpu.VMEM((heads, 2, 2, 2, 32, size), BF16),
            pltpu.VMEM((heads, 2, 2, 2, 32, size), BF16),
            pltpu.VMEM((2, heads, 4, 2, 32, size), BF16),
            pltpu.VMEM((2, heads, 4, 2, 32, size), BF16),
            pltpu.VMEM((2, heads, 4, 2, 32, size), BF16),
            pltpu.VMEM((2, heads, 2, 2, 32, size), BF16),
            pltpu.VMEM((2, heads, 2, 2, 32, size), BF16),
            pltpu.VMEM((heads, 2, 8, 32, size), F32),
            pltpu.VMEM((16, 32, 128), F32),
            pltpu.SemaphoreType.DMA((7,)),
            pltpu.SemaphoreType.DMA((KINDS,)),
            pltpu.SemaphoreType.DMA((KINDS, heads)),
        ],
        compiler_params=pltpu.CompilerParams(
            collective_id=0, has_side_effects=True, vmem_limit_bytes=40 << 20
        ),
    )(*held)
    return pl.pallas_call(
        store,
        out_shape=(shape,) * 4,
        in_specs=[pl.BlockSpec(memory_space=pl.ANY)] * 4,
        out_specs=(hbm,) * 4,
        scratch_shapes=[pltpu.SemaphoreType.DMA((4,))],
        compiler_params=pltpu.CompilerParams(vmem_limit_bytes=1 << 20),
    )(*results)


def solution(mesh):
    cells = P("clip", "ha", "wa", None)
    body = functools.partial(local, mesh.shape["ha"], mesh.shape["wa"])
    return jax.shard_map(
        body,
        mesh=mesh,
        in_specs=(cells,) * 4 + (P(),) * 3,
        out_specs=(cells,) * 4,
        check_vma=False,
    )
```

```python
import functools
import math

import jax
import jax.numpy as jnp
from jax import lax
from jax.experimental import pallas as pl
from jax.experimental.pallas import tpu as pltpu
from jax.sharding import PartitionSpec as P

TILE = 4
SIZES = (1,) * 12
NEG = -1e30
LOG2E = math.log2(math.e)
MESH = pl.DeviceIdType.MESH
F32 = jnp.float32
BF16 = jnp.bfloat16

KINDS = 12
Z_S, Z_N, W_E, W_W, C_E, C_W, GC_E, GC_W, GO_E, GO_W, GH_S, GH_N = range(KINDS)
EARLY = 9
AHEAD = 4
BEHIND = 4
LATE = 6
MEET = 4
WIDE = (1,) * 12
OWNS = (1,) * 12
TILES = (
    (1, 1), (1, 2), (2, 1), (2, 2), (0, 1), (0, 2), (3, 1), (3, 2),
    (1, 0), (2, 0), (0, 0), (3, 0), (1, 3), (2, 3), (0, 3), (3, 3),
)


def split(heads, sizes):
    edges = [0]
    for size in sizes:
        edges.append(min(edges[-1] + size, heads))
    edges += range(edges[-1] + 1, heads + 1)
    return [(a, b) for a, b in zip(edges, edges[1:]) if b > a]


def iota(shape, dim):
    return lax.broadcasted_iota(jnp.int32, shape, dim)


def native_of(a):
    tr, tc, f, r, c = a >> 6, (a >> 5) & 1, (a >> 4) & 1, (a >> 2) & 3, a & 3
    return f * 64 + (tr * 4 + r) * 8 + tc * 4 + c


def dot(a, b, dims):
    return lax.dot_general(a, b, (dims, ((), ())), preferred_element_type=F32)


NT = ((1,), (1,))
NN = ((1,), (0,))
TN = ((0,), (0,))


def kernel(
    heads, n_ha, n_wa,
    q_hbm, k_hbm, v_hbm, g_hbm, win_hbm, vr_hbm, vc_hbm,
    att_ref, dq_ref, dk_ref, dv_ref,
    q_ref, k_ref, v_ref, g_ref, win_ref, vr_ref, vc_ref, own, zin, win, gw, gwr, gh, ghr, acc, kb, load, ready, send, recv,
):
    size = own.shape[-1]
    parts = split(heads, SIZES)
    chunks = len(parts)
    scale = 1.0 / math.sqrt(size)
    ha, wa = lax.axis_index("ha"), lax.axis_index("wa")
    has_n, has_s = ha > 0, ha < n_ha - 1
    has_w, has_e = wa > 0, wa < n_wa - 1
    to_n, to_s = {"ha": ha - 1}, {"ha": ha + 1}
    to_w, to_e = {"wa": wa - 1}, {"wa": wa + 1}

    loads = [
        pltpu.make_async_copy(src, dst, load.at[i])
        for i, (src, dst) in enumerate(
            (
                (k_hbm, k_ref), (v_hbm, v_ref), (q_hbm, q_ref), (g_hbm, g_ref),
                (win_hbm, win_ref), (vr_hbm, vr_ref), (vc_hbm, vc_ref),
            )
        )
    ]
    for copy in loads:
        copy.start()

    barrier = pltpu.get_barrier_semaphore()
    for has, to in ((has_s, to_s), (has_e, to_e)):

        @pl.when(has)
        def _():
            pl.semaphore_signal(barrier, inc=1, device_id=to, device_id_type=MESH)

    @pl.when(has_n | has_w)
    def _():
        pl.semaphore_wait(barrier, has_n.astype(jnp.int32) + has_w.astype(jnp.int32))

    for i, (has, to) in enumerate(((has_n, to_n), (has_w, to_w))):

        @pl.when(has)
        def _():
            pl.semaphore_signal(ready.at[i], inc=1, device_id=to, device_id_type=MESH)

    cells = 128
    perm = jnp.where(native_of(iota((cells, cells), 0)) == iota((cells, cells), 1), 1.0, 0.0)
    perm = perm.astype(BF16)
    back = jnp.where(native_of(iota((cells, cells), 1)) == iota((cells, cells), 0), 1.0, 0.0)
    back = back.astype(BF16)

    def flat(ref, lo, width):
        return ref[:, :, :, lo : lo + width].astype(F32).reshape(cells, width).astype(BF16)

    def permute(c):
        first, last = parts[c]
        for t, ref in enumerate((k_ref, v_ref)):
            width = (last - first) * size
            tiles = dot(perm, flat(ref, first * size, width), NN).astype(BF16)
            for h in range(first, last):
                lo = (h - first) * size
                own[h, :, t] = tiles[:, lo : lo + size].reshape(2, 2, 32, size)

    routes = {
        "n": (to_n, has_n, has_s), "s": (to_s, has_s, has_n),
        "w": (to_w, has_w, has_e), "e": (to_e, has_e, has_w),
    }
    half = {GO_E: slice(0, 2), GO_W: slice(0, 2), GC_E: slice(2, 4), GC_W: slice(2, 4)}

    def ends(kind, at):
        if kind == Z_S:
            return "s", own.at[at, 1], zin.at[at, 0]
        if kind == Z_N:
            return "n", own.at[at, 0], zin.at[at, 1]
        if kind == W_E:
            return "e", own.at[at, :, :, 1], win.at[0, at, 0:2]
        if kind == W_W:
            return "w", own.at[at, :, :, 0], win.at[1, at, 0:2]
        if kind == C_E:
            return "e", zin.at[at, :, :, 1], win.at[0, at, 2:4]
        if kind == C_W:
            return "w", zin.at[at, :, :, 0], win.at[1, at, 2:4]
        if kind in (GC_E, GO_E):
            return "e", gw.at[1, at, half[kind]], gwr.at[0, at, half[kind]]
        if kind in (GC_W, GO_W):
            return "w", gw.at[0, at, half[kind]], gwr.at[1, at, half[kind]]
        if kind == GH_S:
            return "s", gh.at[1, at], ghr.at[0, at]
        return "n", gh.at[0, at], ghr.at[1, at]

    def build(kind, c, part):
        way, src, dst = ends(kind, slice(*part))
        to, sends, gets = routes[way]
        copy = pltpu.make_async_remote_copy(
            src_ref=src, dst_ref=dst, send_sem=send.at[kind], recv_sem=recv.at[kind, c],
            device_id=to, device_id_type=MESH,
        )
        return copy, sends, gets

    cuts = {kind: parts for kind in range(KINDS)}
    cuts[W_E] = cuts[W_W] = split(heads, WIDE)
    cuts[GO_E] = cuts[GO_W] = split(heads, OWNS)
    begun, ended = [0] * KINDS, [0] * KINDS

    def begin(last, *kinds):
        for kind in kinds:
            while begun[kind] < len(cuts[kind]) and cuts[kind][begun[kind]][1] <= last:
                copy, sends, _ = build(kind, begun[kind], cuts[kind][begun[kind]])
                pl.when(sends)(copy.start)
                begun[kind] += 1

    def arrive(last, *kinds):
        for kind in kinds:
            while ended[kind] < len(cuts[kind]) and cuts[kind][ended[kind]][0] < last:
                copy, _, gets = build(kind, ended[kind], cuts[kind][ended[kind]])
                pl.when(gets)(copy.wait_recv)
                ended[kind] += 1

    loads[0].wait()
    loads[1].wait()
    for c in range(chunks):
        permute(c)
        begin(parts[c][1], Z_N)
        begin(min(parts[c][1], EARLY), W_W)
        if c == min(MEET, chunks) - 1:
            for i, has in enumerate((has_s, has_e)):

                @pl.when(has)
                def _():
                    pl.semaphore_wait(ready.at[i], 1)

        if c >= min(MEET, chunks) - 1:
            begin(parts[c][1], Z_S)
            begin(min(parts[c][1], EARLY), W_E)

    def clear(has, ref, *index):
        @pl.when(jnp.logical_not(has))
        def _():
            view = ref.at[index]
            view[...] = jnp.zeros(view.shape, ref.dtype)

    every = slice(None)
    clear(has_n, zin, every, 0)
    clear(has_s, zin, every, 1)
    clear(has_w, win, 0)
    clear(has_e, win, 1)
    clear(has_w, gwr, 0)
    clear(has_e, gwr, 1)
    clear(has_n, ghr, 0)
    clear(has_s, ghr, 1)

    for copy in loads[4:]:
        copy.wait()

    def limits(ref, first):
        count = ref.shape[0]
        out = []
        for e in range(4):
            at = first + e
            inside = (at >= 0) & (at < count)
            out.append(jnp.where(inside, ref[jnp.clip(at, 0, count - 1)], 0))
        return out

    rows, cols = limits(vr_ref, ha * 2 - 1), limits(vc_ref, wa * 2 - 1)
    lane = iota((1, cells), 1)
    lane_r, lane_c = (lane >> 3) & 7, lane & 7
    tile_r, tile_c = (lane_r >> 2) + 1, (lane_c >> 2) + 1
    live = ((lane_r & 3) < jnp.where(tile_r == 1, rows[1], rows[2])) & (
        (lane_c & 3) < jnp.where(tile_c == 1, cols[1], cols[2])
    )
    live = jnp.where(live, 1.0, 0.0).astype(F32)
    sub = iota((32, cells), 0)
    for t, (er, ec) in enumerate(TILES):
        ok = (((sub >> 2) & 3) < rows[er]) & ((sub & 3) < cols[ec])
        kb[t] = jnp.where(ok, 0.0, NEG)

    def attend(h):
        lo = h * size
        w = [win_ref[j, h] for j in range(4)]
        row_bias = [
            jnp.where((e - tile_r >= -w[0]) & (e - tile_r <= w[1]), 0.0, NEG) for e in range(4)
        ]
        col_bias = [
            jnp.where((e - tile_c >= -w[2]) & (e - tile_c <= w[3]), 0.0, NEG) for e in range(4)
        ]
        q = flat(q_ref, lo, size)
        g = flat(g_ref, lo, size)
        key, val = (
            jnp.concatenate(
                [
                    own[h, :, t].reshape(128, size), zin[h, :, t].reshape(128, size),
                    win[0, h, :, t].reshape(128, size), win[1, h, :, t].reshape(128, size),
                ],
                axis=0,
            )
            for t in range(2)
        )
        raw = dot(key, q, NT)
        s = [
            raw[t * 32 : t * 32 + 32] * (scale * LOG2E) + (kb[t] + (row_bias[er] + col_bias[ec]))
            for t, (er, ec) in enumerate(TILES)
        ]
        top = jnp.max(functools.reduce(jnp.maximum, s), axis=0, keepdims=True)
        e = [jnp.exp2(x - top) for x in s]
        total = jnp.sum(sum(e[1:], e[0]), axis=0, keepdims=True)
        inv = live / total
        p = [x * inv for x in e]
        low = [x.astype(BF16) for x in p]
        low_all = jnp.concatenate(low, axis=0)
        raw_d = dot(val, g, NT)
        dp = [raw_d[t * 32 : t * 32 + 32] for t in range(16)]
        prod = [a.astype(F32) * b for a, b in zip(low, dp)]
        dots = jnp.sum(sum(prod[1:], prod[0]), axis=0, keepdims=True)
        ds = jnp.concatenate([(a * (b - dots)).astype(BF16) for a, b in zip(p, dp)], axis=0)
        dk = dot(ds, q, NN) * scale
        dv = dot(low_all, g, NN)
        for t, part in enumerate((dk, dv)):
            acc[h, t] = part[0:256].reshape(8, 32, size)
            for side in range(2):
                rim = part[256 + side * 128 : 384 + side * 128]
                gw[side, h, :, t] = rim.reshape(4, 32, size).astype(BF16)

        def finish():
            out = dot(low_all, val, TN)
            att_ref[:, :, :, lo : lo + size] = out.reshape(2, 8, 8, size).astype(BF16)
            dq = dot(ds, key, TN) * scale
            dq_ref[:, :, :, lo : lo + size] = dq.reshape(2, 8, 8, size).astype(BF16)

        return finish

    def fold_width(c):
        arrive(parts[c][1], GC_E, GC_W)
        for h in range(*parts[c]):
            for t in range(2):
                for ns in range(2):
                    for col in range(2):
                        both = acc[h, t, 4 + ns * 2 + col] + gwr[col, h, 2 + ns, t].astype(F32)
                        gh[ns, h, t, col] = both.astype(BF16)
        begin(parts[c][1], GH_S, GH_N)

    def fold_height(c):
        arrive(parts[c][1], GO_E, GO_W, GH_S, GH_N)
        for t, ref in enumerate((dk_ref, dv_ref)):
            both = []
            for h in range(*parts[c]):
                tiles = [
                    acc[h, t, r * 2 + col] + ghr[r, h, t, col].astype(F32) + gwr[col, h, r, t].astype(F32)
                    for r in range(2)
                    for col in range(2)
                ]
                both.append(jnp.concatenate(tiles, axis=0).astype(BF16))
            lo, width = parts[c][0] * size, len(both) * size
            grid = dot(back, jnp.concatenate(both, axis=1), NN)
            ref[:, :, :, lo : lo + width] = grid.reshape(2, 8, 8, width).astype(BF16)

    def forward(c):
        arrive(parts[c][1], Z_S, Z_N)
        begin(parts[c][1], C_E, C_W)
        begin(parts[c][1] + EARLY, W_E, W_W)

    for c in range(min(AHEAD, chunks)):
        forward(c)
    loads[2].wait()
    loads[3].wait()
    for step in range(chunks):
        if step + AHEAD < chunks:
            forward(step + AHEAD)
        arrive(parts[step][1], W_E, W_W, C_E, C_W)
        rest = [attend(h) for h in range(*parts[step])]
        begin(parts[step][1], GC_E, GC_W)
        for finish in rest:
            finish()
        if step >= BEHIND:
            fold_width(step - BEHIND)
        begin(parts[step][1] - LATE, GO_E, GO_W)
    for c in range(max(chunks - BEHIND, 0), chunks):
        fold_width(c)
        begin(parts[c][1], GO_E, GO_W)
    for c in range(chunks):
        fold_height(c)

    for kind in range(KINDS):
        copy, sends, _ = build(kind, 0, (0, heads))
        pl.when(sends)(copy.wait_send)


def store(*refs):
    sem = refs[-1]
    count = len(refs) // 2
    copies = [
        pltpu.make_async_copy(refs[i], refs[count + i], sem.at[i]) for i in range(count)
    ]
    for copy in copies:
        copy.start()
    for copy in copies:
        copy.wait()


def local(n_ha, n_wa, queries, keys, values, out_grad, windows, valid_rows, valid_cols):
    heads = windows.shape[0]
    size = queries.shape[-1] // heads
    vmem = pl.BlockSpec(memory_space=pltpu.VMEM)
    hbm = pl.BlockSpec(memory_space=pltpu.HBM)
    shape = jax.ShapeDtypeStruct(queries.shape, BF16)
    held = [
        pltpu.with_memory_space_constraint(x, pltpu.HBM)
        for x in (queries, keys, values, out_grad, windows.T, valid_rows, valid_cols)
    ]
    results = pl.pallas_call(
        functools.partial(kernel, heads, n_ha, n_wa),
        out_shape=(shape,) * 4,
        in_specs=[hbm] * 7,
        out_specs=(vmem,) * 4,
        scratch_shapes=[pltpu.VMEM(queries.shape, BF16)] * 4
        + [
            pltpu.SMEM((4, heads), jnp.int32),
            pltpu.SMEM(valid_rows.shape, jnp.int32),
            pltpu.SMEM(valid_cols.shape, jnp.int32),
            pltpu.VMEM((heads, 2, 2, 2, 32, size), BF16),
            pltpu.VMEM((heads, 2, 2, 2, 32, size), BF16),
            pltpu.VMEM((2, heads, 4, 2, 32, size), BF16),
            pltpu.VMEM((2, heads, 4, 2, 32, size), BF16),
            pltpu.VMEM((2, heads, 4, 2, 32, size), BF16),
            pltpu.VMEM((2, heads, 2, 2, 32, size), BF16),
            pltpu.VMEM((2, heads, 2, 2, 32, size), BF16),
            pltpu.VMEM((heads, 2, 8, 32, size), F32),
            pltpu.VMEM((16, 32, 128), F32),
            pltpu.SemaphoreType.DMA((7,)),
            pltpu.SemaphoreType.REGULAR((2,)),
            pltpu.SemaphoreType.DMA((KINDS,)),
            pltpu.SemaphoreType.DMA((KINDS, heads)),
        ],
        compiler_params=pltpu.CompilerParams(
            collective_id=0, has_side_effects=True, vmem_limit_bytes=40 << 20
        ),
    )(*held)
    return pl.pallas_call(
        store,
        out_shape=(shape,) * 4,
        in_specs=[pl.BlockSpec(memory_space=pl.ANY)] * 4,
        out_specs=(hbm,) * 4,
        scratch_shapes=[pltpu.SemaphoreType.DMA((4,))],
        compiler_params=pltpu.CompilerParams(vmem_limit_bytes=1 << 20),
    )(*results)


def solution(mesh):
    cells = P("clip", "ha", "wa", None)
    body = functools.partial(local, mesh.shape["ha"], mesh.shape["wa"])
    return jax.shard_map(
        body,
        mesh=mesh,
        in_specs=(cells,) * 4 + (P(),) * 3,
        out_specs=(cells,) * 4,
        check_vma=False,
    )
```

```python
import functools
import math

import jax
import jax.numpy as jnp
from jax import lax
from jax.experimental import pallas as pl
from jax.experimental.pallas import tpu as pltpu
from jax.sharding import PartitionSpec as P

TILE = 4
SIZES = (1,) * 12
NEG = -1e30
LOG2E = math.log2(math.e)
MESH = pl.DeviceIdType.MESH
F32 = jnp.float32
BF16 = jnp.bfloat16

KINDS = 12
Z_S, Z_N, W_E, W_W, C_E, C_W, GC_E, GC_W, GO_E, GO_W, GH_S, GH_N = range(KINDS)
EARLY = 9
AHEAD = 4
BEHIND = 4
NEAR = 3
FIRST = 2
LATE = 6
MEET = 2
WIDE = (1,) * 12
OWNS = (1,) * 12
TILES = (
    (1, 1), (1, 2), (2, 1), (2, 2), (0, 1), (0, 2), (3, 1), (3, 2),
    (1, 0), (2, 0), (0, 0), (3, 0), (1, 3), (2, 3), (0, 3), (3, 3),
)


def split(heads, sizes):
    edges = [0]
    for size in sizes:
        edges.append(min(edges[-1] + size, heads))
    edges += range(edges[-1] + 1, heads + 1)
    return [(a, b) for a, b in zip(edges, edges[1:]) if b > a]


def iota(shape, dim):
    return lax.broadcasted_iota(jnp.int32, shape, dim)


def native_of(a):
    tr, tc, f, r, c = a >> 6, (a >> 5) & 1, (a >> 4) & 1, (a >> 2) & 3, a & 3
    return f * 64 + (tr * 4 + r) * 8 + tc * 4 + c


def dot(a, b, dims):
    return lax.dot_general(a, b, (dims, ((), ())), preferred_element_type=F32)


NT = ((1,), (1,))
NN = ((1,), (0,))
TN = ((0,), (0,))


def kernel(
    heads, n_ha, n_wa,
    q_hbm, k_hbm, v_hbm, g_hbm, win_hbm, vr_hbm, vc_hbm,
    att_ref, dq_ref, dk_ref, dv_ref,
    q_ref, k_ref, v_ref, g_ref, win_ref, vr_ref, vc_ref, own, zin, win, gw, gwr, gh, ghr, acc, kb, load, ready, send, recv,
):
    size = own.shape[-1]
    parts = split(heads, SIZES)
    chunks = len(parts)
    scale = 1.0 / math.sqrt(size)
    ha, wa = lax.axis_index("ha"), lax.axis_index("wa")
    has_n, has_s = ha > 0, ha < n_ha - 1
    has_w, has_e = wa > 0, wa < n_wa - 1
    to_n, to_s = {"ha": ha - 1}, {"ha": ha + 1}
    to_w, to_e = {"wa": wa - 1}, {"wa": wa + 1}

    cut = FIRST * size
    feats = q_ref.shape[-1]

    def lanes(src, dst, lo, hi):
        at = (slice(None), slice(None), slice(None), slice(lo, hi))
        return src.at[at], dst.at[at]

    loads = [
        pltpu.make_async_copy(src, dst, load.at[i])
        for i, (src, dst) in enumerate(
            (
                lanes(k_hbm, k_ref, 0, cut), lanes(v_hbm, v_ref, 0, cut),
                lanes(k_hbm, k_ref, cut, feats), lanes(v_hbm, v_ref, cut, feats),
                (win_hbm, win_ref), (vr_hbm, vr_ref), (vc_hbm, vc_ref),
                (q_hbm, q_ref), (g_hbm, g_ref),
            )
        )
    ]
    for copy in loads:
        copy.start()

    barrier = pltpu.get_barrier_semaphore()
    for has, to in ((has_s, to_s), (has_e, to_e)):

        @pl.when(has)
        def _():
            pl.semaphore_signal(barrier, inc=1, device_id=to, device_id_type=MESH)

    @pl.when(has_n | has_w)
    def _():
        pl.semaphore_wait(barrier, has_n.astype(jnp.int32) + has_w.astype(jnp.int32))

    for i, (has, to) in enumerate(((has_n, to_n), (has_w, to_w))):

        @pl.when(has)
        def _():
            pl.semaphore_signal(ready.at[i], inc=1, device_id=to, device_id_type=MESH)

    cells = 128
    perm = jnp.where(native_of(iota((cells, cells), 0)) == iota((cells, cells), 1), 1.0, 0.0)
    perm = perm.astype(BF16)
    back = jnp.where(native_of(iota((cells, cells), 1)) == iota((cells, cells), 0), 1.0, 0.0)
    back = back.astype(BF16)

    def flat(ref, lo, width):
        return ref[:, :, :, lo : lo + width].astype(F32).reshape(cells, width).astype(BF16)

    def permute(c):
        first, last = parts[c]
        for t, ref in enumerate((k_ref, v_ref)):
            width = (last - first) * size
            tiles = dot(perm, flat(ref, first * size, width), NN).astype(BF16)
            for h in range(first, last):
                lo = (h - first) * size
                own[h, :, t] = tiles[:, lo : lo + size].reshape(2, 2, 32, size)

    routes = {
        "n": (to_n, has_n, has_s), "s": (to_s, has_s, has_n),
        "w": (to_w, has_w, has_e), "e": (to_e, has_e, has_w),
    }
    half = {GO_E: slice(0, 2), GO_W: slice(0, 2), GC_E: slice(2, 4), GC_W: slice(2, 4)}

    def ends(kind, at):
        if kind == Z_S:
            return "s", own.at[at, 1], zin.at[at, 0]
        if kind == Z_N:
            return "n", own.at[at, 0], zin.at[at, 1]
        if kind == W_E:
            return "e", own.at[at, :, :, 1], win.at[0, at, 0:2]
        if kind == W_W:
            return "w", own.at[at, :, :, 0], win.at[1, at, 0:2]
        if kind == C_E:
            return "e", zin.at[at, :, :, 1], win.at[0, at, 2:4]
        if kind == C_W:
            return "w", zin.at[at, :, :, 0], win.at[1, at, 2:4]
        if kind in (GC_E, GO_E):
            return "e", gw.at[1, at, half[kind]], gwr.at[0, at, half[kind]]
        if kind in (GC_W, GO_W):
            return "w", gw.at[0, at, half[kind]], gwr.at[1, at, half[kind]]
        if kind == GH_S:
            return "s", gh.at[1, at], ghr.at[0, at]
        return "n", gh.at[0, at], ghr.at[1, at]

    def build(kind, c, part):
        way, src, dst = ends(kind, slice(*part))
        to, sends, gets = routes[way]
        copy = pltpu.make_async_remote_copy(
            src_ref=src, dst_ref=dst, send_sem=send.at[kind], recv_sem=recv.at[kind, c],
            device_id=to, device_id_type=MESH,
        )
        return copy, sends, gets

    cuts = {kind: parts for kind in range(KINDS)}
    cuts[W_E] = cuts[W_W] = split(heads, WIDE)
    cuts[GO_E] = cuts[GO_W] = split(heads, OWNS)
    begun, ended = [0] * KINDS, [0] * KINDS

    def begin(last, *kinds):
        for kind in kinds:
            while begun[kind] < len(cuts[kind]) and cuts[kind][begun[kind]][1] <= last:
                copy, sends, _ = build(kind, begun[kind], cuts[kind][begun[kind]])
                pl.when(sends)(copy.start)
                begun[kind] += 1

    def arrive(last, *kinds):
        for kind in kinds:
            while ended[kind] < len(cuts[kind]) and cuts[kind][ended[kind]][0] < last:
                copy, _, gets = build(kind, ended[kind], cuts[kind][ended[kind]])
                pl.when(gets)(copy.wait_recv)
                ended[kind] += 1

    loads[0].wait()
    loads[1].wait()
    for c in range(chunks):
        if c == FIRST:
            loads[2].wait()
            loads[3].wait()
        permute(c)
        begin(parts[c][1], Z_N)
        begin(min(parts[c][1], EARLY), W_W)
        if c == min(MEET, chunks) - 1:
            for i, has in enumerate((has_s, has_e)):

                @pl.when(has)
                def _():
                    pl.semaphore_wait(ready.at[i], 1)

        if c >= min(MEET, chunks) - 1:
            begin(parts[c][1], Z_S)
            begin(min(parts[c][1], EARLY), W_E)

    def clear(has, ref, *index):
        @pl.when(jnp.logical_not(has))
        def _():
            view = ref.at[index]
            view[...] = jnp.zeros(view.shape, ref.dtype)

    every = slice(None)
    clear(has_n, zin, every, 0)
    clear(has_s, zin, every, 1)
    clear(has_w, win, 0)
    clear(has_e, win, 1)
    clear(has_w, gwr, 0)
    clear(has_e, gwr, 1)
    clear(has_n, ghr, 0)
    clear(has_s, ghr, 1)

    for copy in loads[4:7]:
        copy.wait()

    def limits(ref, first):
        count = ref.shape[0]
        out = []
        for e in range(4):
            at = first + e
            inside = (at >= 0) & (at < count)
            out.append(jnp.where(inside, ref[jnp.clip(at, 0, count - 1)], 0))
        return out

    rows, cols = limits(vr_ref, ha * 2 - 1), limits(vc_ref, wa * 2 - 1)
    lane = iota((1, cells), 1)
    lane_r, lane_c = (lane >> 3) & 7, lane & 7
    tile_r, tile_c = (lane_r >> 2) + 1, (lane_c >> 2) + 1
    live = ((lane_r & 3) < jnp.where(tile_r == 1, rows[1], rows[2])) & (
        (lane_c & 3) < jnp.where(tile_c == 1, cols[1], cols[2])
    )
    live = jnp.where(live, 1.0, 0.0).astype(F32)
    sub = iota((32, cells), 0)
    for t, (er, ec) in enumerate(TILES):
        ok = (((sub >> 2) & 3) < rows[er]) & ((sub & 3) < cols[ec])
        kb[t] = jnp.where(ok, 0.0, NEG)

    def attend(h):
        lo = h * size
        w = [win_ref[j, h] for j in range(4)]
        row_bias = [
            jnp.where((e - tile_r >= -w[0]) & (e - tile_r <= w[1]), 0.0, NEG) for e in range(4)
        ]
        col_bias = [
            jnp.where((e - tile_c >= -w[2]) & (e - tile_c <= w[3]), 0.0, NEG) for e in range(4)
        ]
        q = flat(q_ref, lo, size)
        g = flat(g_ref, lo, size)
        key, val = (
            jnp.concatenate(
                [
                    own[h, :, t].reshape(128, size), zin[h, :, t].reshape(128, size),
                    win[0, h, :, t].reshape(128, size), win[1, h, :, t].reshape(128, size),
                ],
                axis=0,
            )
            for t in range(2)
        )
        raw = dot(key, q, NT)
        s = [
            raw[t * 32 : t * 32 + 32] * (scale * LOG2E) + (kb[t] + (row_bias[er] + col_bias[ec]))
            for t, (er, ec) in enumerate(TILES)
        ]
        top = jnp.max(functools.reduce(jnp.maximum, s), axis=0, keepdims=True)
        e = [jnp.exp2(x - top) for x in s]
        total = jnp.sum(sum(e[1:], e[0]), axis=0, keepdims=True)
        inv = live / total
        p = [x * inv for x in e]
        low = [x.astype(BF16) for x in p]
        low_all = jnp.concatenate(low, axis=0)
        raw_d = dot(val, g, NT)
        dp = [raw_d[t * 32 : t * 32 + 32] for t in range(16)]
        prod = [a.astype(F32) * b for a, b in zip(low, dp)]
        dots = jnp.sum(sum(prod[1:], prod[0]), axis=0, keepdims=True)
        ds = jnp.concatenate([(a * (b - dots)).astype(BF16) for a, b in zip(p, dp)], axis=0)
        dk = dot(ds, q, NN) * scale
        dv = dot(low_all, g, NN)
        for t, part in enumerate((dk, dv)):
            acc[h, t] = part[0:256].reshape(8, 32, size)
            for side in range(2):
                rim = part[256 + side * 128 : 384 + side * 128]
                gw[side, h, :, t] = rim.reshape(4, 32, size).astype(BF16)

        def finish():
            out = dot(low_all, val, TN)
            att_ref[:, :, :, lo : lo + size] = out.reshape(2, 8, 8, size).astype(BF16)
            dq = dot(ds, key, TN) * scale
            dq_ref[:, :, :, lo : lo + size] = dq.reshape(2, 8, 8, size).astype(BF16)

        return finish

    rim = (wa == 0) | (wa == n_wa - 1)
    middle = jnp.logical_not(rim)

    def fold_width(c, who):
        for kind in (GC_E, GC_W):
            copy, _, gets = build(kind, c, parts[c])
            pl.when(gets & who)(copy.wait_recv)

        @pl.when(who)
        def _():
            for h in range(*parts[c]):
                for t in range(2):
                    for ns in range(2):
                        for col in range(2):
                            both = acc[h, t, 4 + ns * 2 + col] + gwr[col, h, 2 + ns, t].astype(F32)
                            gh[ns, h, t, col] = both.astype(BF16)

        for kind in (GH_S, GH_N):
            copy, sends, _ = build(kind, c, parts[c])
            pl.when(sends & who)(copy.start)

    def fold_height(c):
        arrive(parts[c][1], GO_E, GO_W, GH_S, GH_N)
        for t, ref in enumerate((dk_ref, dv_ref)):
            both = []
            for h in range(*parts[c]):
                tiles = [
                    acc[h, t, r * 2 + col] + ghr[r, h, t, col].astype(F32) + gwr[col, h, r, t].astype(F32)
                    for r in range(2)
                    for col in range(2)
                ]
                both.append(jnp.concatenate(tiles, axis=0).astype(BF16))
            lo, width = parts[c][0] * size, len(both) * size
            grid = dot(back, jnp.concatenate(both, axis=1), NN)
            ref[:, :, :, lo : lo + width] = grid.reshape(2, 8, 8, width).astype(BF16)

    def forward(c):
        arrive(parts[c][1], Z_S, Z_N)
        begin(parts[c][1], C_E, C_W)
        begin(parts[c][1] + EARLY, W_E, W_W)

    for c in range(min(AHEAD, chunks)):
        forward(c)
    loads[7].wait()
    loads[8].wait()
    for step in range(chunks):
        if step + AHEAD < chunks:
            forward(step + AHEAD)
        arrive(parts[step][1], W_E, W_W, C_E, C_W)
        rest = [attend(h) for h in range(*parts[step])]
        begin(parts[step][1], GC_E, GC_W)
        for finish in rest:
            finish()
        if step >= BEHIND:
            fold_width(step - BEHIND, middle)
        if step >= NEAR:
            fold_width(step - NEAR, rim)
        begin(parts[step][1] - LATE, GO_E, GO_W)
    for c in range(max(chunks - NEAR, 0), chunks):
        fold_width(c, rim)
    for c in range(max(chunks - BEHIND, 0), chunks):
        fold_width(c, middle)
        begin(parts[c][1], GO_E, GO_W)
    for c in range(chunks):
        fold_height(c)

    for kind in range(KINDS):
        copy, sends, _ = build(kind, 0, (0, heads))
        pl.when(sends)(copy.wait_send)


def store(*refs):
    sem = refs[-1]
    count = len(refs) // 2
    copies = [
        pltpu.make_async_copy(refs[i], refs[count + i], sem.at[i]) for i in range(count)
    ]
    for copy in copies:
        copy.start()
    for copy in copies:
        copy.wait()


def local(n_ha, n_wa, queries, keys, values, out_grad, windows, valid_rows, valid_cols):
    heads = windows.shape[0]
    size = queries.shape[-1] // heads
    vmem = pl.BlockSpec(memory_space=pltpu.VMEM)
    hbm = pl.BlockSpec(memory_space=pltpu.HBM)
    shape = jax.ShapeDtypeStruct(queries.shape, BF16)
    held = [
        pltpu.with_memory_space_constraint(x, pltpu.HBM)
        for x in (queries, keys, values, out_grad, windows.T, valid_rows, valid_cols)
    ]
    results = pl.pallas_call(
        functools.partial(kernel, heads, n_ha, n_wa),
        out_shape=(shape,) * 4,
        in_specs=[hbm] * 7,
        out_specs=(vmem,) * 4,
        scratch_shapes=[pltpu.VMEM(queries.shape, BF16)] * 4
        + [
            pltpu.SMEM((4, heads), jnp.int32),
            pltpu.SMEM(valid_rows.shape, jnp.int32),
            pltpu.SMEM(valid_cols.shape, jnp.int32),
            pltpu.VMEM((heads, 2, 2, 2, 32, size), BF16),
            pltpu.VMEM((heads, 2, 2, 2, 32, size), BF16),
            pltpu.VMEM((2, heads, 4, 2, 32, size), BF16),
            pltpu.VMEM((2, heads, 4, 2, 32, size), BF16),
            pltpu.VMEM((2, heads, 4, 2, 32, size), BF16),
            pltpu.VMEM((2, heads, 2, 2, 32, size), BF16),
            pltpu.VMEM((2, heads, 2, 2, 32, size), BF16),
            pltpu.VMEM((heads, 2, 8, 32, size), F32),
            pltpu.VMEM((16, 32, 128), F32),
            pltpu.SemaphoreType.DMA((9,)),
            pltpu.SemaphoreType.REGULAR((2,)),
            pltpu.SemaphoreType.DMA((KINDS,)),
            pltpu.SemaphoreType.DMA((KINDS, heads)),
        ],
        compiler_params=pltpu.CompilerParams(
            collective_id=0, has_side_effects=True, vmem_limit_bytes=40 << 20
        ),
    )(*held)
    return pl.pallas_call(
        store,
        out_shape=(shape,) * 4,
        in_specs=[pl.BlockSpec(memory_space=pl.ANY)] * 4,
        out_specs=(hbm,) * 4,
        scratch_shapes=[pltpu.SemaphoreType.DMA((4,))],
        compiler_params=pltpu.CompilerParams(vmem_limit_bytes=1 << 20),
    )(*results)


def solution(mesh):
    cells = P("clip", "ha", "wa", None)
    body = functools.partial(local, mesh.shape["ha"], mesh.shape["wa"])
    return jax.shard_map(
        body,
        mesh=mesh,
        in_specs=(cells,) * 4 + (P(),) * 3,
        out_specs=(cells,) * 4,
        check_vma=False,
    )
```

```python
import functools
import math

import jax
import jax.numpy as jnp
from jax import lax
from jax.experimental import pallas as pl
from jax.experimental.pallas import tpu as pltpu
from jax.sharding import PartitionSpec as P

TILE = 4
SIZES = (1,) * 12
NEG = -1e30
LOG2E = math.log2(math.e)
MESH = pl.DeviceIdType.MESH
F32 = jnp.float32
BF16 = jnp.bfloat16

KINDS = 12
Z_S, Z_N, W_E, W_W, C_E, C_W, GC_E, GC_W, GO_E, GO_W, GH_S, GH_N = range(KINDS)
EARLY = 9
AHEAD = 4
BEHIND = 4
NEAR = 3
FIRST = 2
LATE = 7
MEET = 2
WIDE = (1,) * 12
OWNS = (1,) * 12
TILES = (
    (1, 1), (1, 2), (2, 1), (2, 2), (0, 1), (0, 2), (3, 1), (3, 2),
    (1, 0), (2, 0), (1, 3), (2, 3), (0, 0), (3, 0), (0, 3), (3, 3),
)


def split(heads, sizes):
    edges = [0]
    for size in sizes:
        edges.append(min(edges[-1] + size, heads))
    edges += range(edges[-1] + 1, heads + 1)
    return [(a, b) for a, b in zip(edges, edges[1:]) if b > a]


def iota(shape, dim):
    return lax.broadcasted_iota(jnp.int32, shape, dim)


def native_of(a):
    tr, tc, f, r, c = a >> 6, (a >> 5) & 1, (a >> 4) & 1, (a >> 2) & 3, a & 3
    return f * 64 + (tr * 4 + r) * 8 + tc * 4 + c


def dot(a, b, dims):
    return lax.dot_general(a, b, (dims, ((), ())), preferred_element_type=F32)


NT = ((1,), (1,))
NN = ((1,), (0,))
TN = ((0,), (0,))


def kernel(
    heads, n_ha, n_wa,
    q_hbm, k_hbm, v_hbm, g_hbm, win_hbm, vr_hbm, vc_hbm,
    att_ref, dq_ref, dk_ref, dv_ref,
    q_ref, k_ref, v_ref, g_ref, win_ref, vr_ref, vc_ref, own, zin, win, gw, gwr, gh, ghr, acc, kb, load, ready, send, recv,
):
    size = own.shape[-1]
    parts = split(heads, SIZES)
    chunks = len(parts)
    scale = 1.0 / math.sqrt(size)
    ha, wa = lax.axis_index("ha"), lax.axis_index("wa")
    has_n, has_s = ha > 0, ha < n_ha - 1
    has_w, has_e = wa > 0, wa < n_wa - 1
    to_n, to_s = {"ha": ha - 1}, {"ha": ha + 1}
    to_w, to_e = {"wa": wa - 1}, {"wa": wa + 1}

    cut = FIRST * size
    feats = q_ref.shape[-1]

    def lanes(src, dst, lo, hi):
        at = (slice(None), slice(None), slice(None), slice(lo, hi))
        return src.at[at], dst.at[at]

    loads = [
        pltpu.make_async_copy(src, dst, load.at[i])
        for i, (src, dst) in enumerate(
            (
                lanes(k_hbm, k_ref, 0, cut), lanes(v_hbm, v_ref, 0, cut),
                lanes(k_hbm, k_ref, cut, feats), lanes(v_hbm, v_ref, cut, feats),
                (win_hbm, win_ref), (vr_hbm, vr_ref), (vc_hbm, vc_ref),
                (q_hbm, q_ref), (g_hbm, g_ref),
            )
        )
    ]
    for copy in loads:
        copy.start()

    barrier = pltpu.get_barrier_semaphore()
    for has, to in ((has_s, to_s), (has_e, to_e)):

        @pl.when(has)
        def _():
            pl.semaphore_signal(barrier, inc=1, device_id=to, device_id_type=MESH)

    @pl.when(has_n | has_w)
    def _():
        pl.semaphore_wait(barrier, has_n.astype(jnp.int32) + has_w.astype(jnp.int32))

    for i, (has, to) in enumerate(((has_n, to_n), (has_w, to_w))):

        @pl.when(has)
        def _():
            pl.semaphore_signal(ready.at[i], inc=1, device_id=to, device_id_type=MESH)

    cells = 128
    perm = jnp.where(native_of(iota((cells, cells), 0)) == iota((cells, cells), 1), 1.0, 0.0)
    perm = perm.astype(BF16)
    back = jnp.where(native_of(iota((cells, cells), 1)) == iota((cells, cells), 0), 1.0, 0.0)
    back = back.astype(BF16)

    def flat(ref, lo, width):
        return ref[:, :, :, lo : lo + width].astype(F32).reshape(cells, width).astype(BF16)

    def permute(c):
        first, last = parts[c]
        for t, ref in enumerate((k_ref, v_ref)):
            width = (last - first) * size
            tiles = dot(perm, flat(ref, first * size, width), NN).astype(BF16)
            for h in range(first, last):
                lo = (h - first) * size
                own[h, :, t] = tiles[:, lo : lo + size].reshape(2, 2, 32, size)

    routes = {
        "n": (to_n, has_n, has_s), "s": (to_s, has_s, has_n),
        "w": (to_w, has_w, has_e), "e": (to_e, has_e, has_w),
    }
    half = {GO_E: slice(0, 2), GO_W: slice(0, 2), GC_E: slice(2, 4), GC_W: slice(2, 4)}

    def ends(kind, at):
        if kind == Z_S:
            return "s", own.at[at, 1], zin.at[at, 0]
        if kind == Z_N:
            return "n", own.at[at, 0], zin.at[at, 1]
        if kind == W_E:
            return "e", own.at[at, :, :, 1], win.at[0, at, 0:2]
        if kind == W_W:
            return "w", own.at[at, :, :, 0], win.at[1, at, 0:2]
        if kind == C_E:
            return "e", zin.at[at, :, :, 1], win.at[0, at, 2:4]
        if kind == C_W:
            return "w", zin.at[at, :, :, 0], win.at[1, at, 2:4]
        if kind in (GC_E, GO_E):
            return "e", gw.at[1, at, half[kind]], gwr.at[0, at, half[kind]]
        if kind in (GC_W, GO_W):
            return "w", gw.at[0, at, half[kind]], gwr.at[1, at, half[kind]]
        if kind == GH_S:
            return "s", gh.at[1, at], ghr.at[0, at]
        return "n", gh.at[0, at], ghr.at[1, at]

    def build(kind, c, part):
        way, src, dst = ends(kind, slice(*part))
        to, sends, gets = routes[way]
        copy = pltpu.make_async_remote_copy(
            src_ref=src, dst_ref=dst, send_sem=send.at[kind], recv_sem=recv.at[kind, c],
            device_id=to, device_id_type=MESH,
        )
        return copy, sends, gets

    cuts = {kind: parts for kind in range(KINDS)}
    cuts[W_E] = cuts[W_W] = split(heads, WIDE)
    cuts[GO_E] = cuts[GO_W] = split(heads, OWNS)
    begun, ended = [0] * KINDS, [0] * KINDS

    def begin(last, *kinds):
        for kind in kinds:
            while begun[kind] < len(cuts[kind]) and cuts[kind][begun[kind]][1] <= last:
                copy, sends, _ = build(kind, begun[kind], cuts[kind][begun[kind]])
                pl.when(sends)(copy.start)
                begun[kind] += 1

    def arrive(last, *kinds):
        for kind in kinds:
            while ended[kind] < len(cuts[kind]) and cuts[kind][ended[kind]][0] < last:
                copy, _, gets = build(kind, ended[kind], cuts[kind][ended[kind]])
                pl.when(gets)(copy.wait_recv)
                ended[kind] += 1

    loads[0].wait()
    loads[1].wait()
    for c in range(chunks):
        if c == FIRST:
            loads[2].wait()
            loads[3].wait()
        permute(c)
        begin(parts[c][1], Z_N)
        begin(min(parts[c][1], EARLY), W_W)
        if c == min(MEET, chunks) - 1:
            for i, has in enumerate((has_s, has_e)):

                @pl.when(has)
                def _():
                    pl.semaphore_wait(ready.at[i], 1)

        if c >= min(MEET, chunks) - 1:
            begin(parts[c][1], Z_S)
            begin(min(parts[c][1], EARLY), W_E)

    def clear(has, ref, *index):
        @pl.when(jnp.logical_not(has))
        def _():
            view = ref.at[index]
            view[...] = jnp.zeros(view.shape, ref.dtype)

    every = slice(None)
    clear(has_n, zin, every, 0)
    clear(has_s, zin, every, 1)
    clear(has_w, win, 0)
    clear(has_e, win, 1)
    clear(has_w, gwr, 0)
    clear(has_e, gwr, 1)
    clear(has_n, ghr, 0)
    clear(has_s, ghr, 1)

    for copy in loads[4:7]:
        copy.wait()

    def limits(ref, first):
        count = ref.shape[0]
        out = []
        for e in range(4):
            at = first + e
            inside = (at >= 0) & (at < count)
            out.append(jnp.where(inside, ref[jnp.clip(at, 0, count - 1)], 0))
        return out

    rows, cols = limits(vr_ref, ha * 2 - 1), limits(vc_ref, wa * 2 - 1)
    lane = iota((1, cells), 1)
    lane_r, lane_c = (lane >> 3) & 7, lane & 7
    tile_r, tile_c = (lane_r >> 2) + 1, (lane_c >> 2) + 1
    live = ((lane_r & 3) < jnp.where(tile_r == 1, rows[1], rows[2])) & (
        (lane_c & 3) < jnp.where(tile_c == 1, cols[1], cols[2])
    )
    live = jnp.where(live, 1.0, 0.0).astype(F32)
    sub = iota((32, cells), 0)
    for t, (er, ec) in enumerate(TILES):
        ok = (((sub >> 2) & 3) < rows[er]) & ((sub & 3) < cols[ec])
        kb[t] = jnp.where(ok, 0.0, NEG)

    def attend(h):
        lo = h * size
        w = [win_ref[j, h] for j in range(4)]
        row_bias = [
            jnp.where((e - tile_r >= -w[0]) & (e - tile_r <= w[1]), 0.0, NEG) for e in range(4)
        ]
        col_bias = [
            jnp.where((e - tile_c >= -w[2]) & (e - tile_c <= w[3]), 0.0, NEG) for e in range(4)
        ]
        q = flat(q_ref, lo, size)
        g = flat(g_ref, lo, size)
        key, val = (
            jnp.concatenate(
                [
                    own[h, :, t].reshape(128, size), zin[h, :, t].reshape(128, size),
                    win[0, h, 0:2, t].reshape(64, size), win[1, h, 0:2, t].reshape(64, size),
                    win[0, h, 2:4, t].reshape(64, size), win[1, h, 2:4, t].reshape(64, size),
                ],
                axis=0,
            )
            for t in range(2)
        )
        raw = dot(key, q, NT)
        s = [
            raw[t * 32 : t * 32 + 32] * (scale * LOG2E) + (kb[t] + (row_bias[er] + col_bias[ec]))
            for t, (er, ec) in enumerate(TILES)
        ]
        top = jnp.max(functools.reduce(jnp.maximum, s), axis=0, keepdims=True)
        e = [jnp.exp2(x - top) for x in s]
        total = jnp.sum(sum(e[1:], e[0]), axis=0, keepdims=True)
        inv = live / total
        p = [x * inv for x in e]
        low = [x.astype(BF16) for x in p]
        low_all = jnp.concatenate(low, axis=0)
        raw_d = dot(val, g, NT)
        dp = [raw_d[t * 32 : t * 32 + 32] for t in range(16)]
        prod = [a.astype(F32) * b for a, b in zip(low, dp)]
        dots = jnp.sum(sum(prod[1:], prod[0]), axis=0, keepdims=True)
        ds = jnp.concatenate([(a * (b - dots)).astype(BF16) for a, b in zip(p, dp)], axis=0)
        for t, (left, right) in enumerate(((ds, q), (low_all, g))):
            part = dot(left[384:512], right, NN)
            if t == 0:
                part = part * scale
            part = part.reshape(2, 2, 32, size).astype(BF16)
            for side in range(2):
                gw[side, h, 2:4, t] = part[side]

        def finish():
            for t, (left, right) in enumerate(((ds, q), (low_all, g))):
                part = dot(left[0:384], right, NN)
                if t == 0:
                    part = part * scale
                acc[h, t] = part[0:256].reshape(8, 32, size)
                for side in range(2):
                    rim = part[256 + side * 64 : 320 + side * 64]
                    gw[side, h, 0:2, t] = rim.reshape(2, 32, size).astype(BF16)
            out = dot(low_all, val, TN)
            att_ref[:, :, :, lo : lo + size] = out.reshape(2, 8, 8, size).astype(BF16)
            dq = dot(ds, key, TN) * scale
            dq_ref[:, :, :, lo : lo + size] = dq.reshape(2, 8, 8, size).astype(BF16)

        return finish

    rim = (wa == 0) | (wa == n_wa - 1)
    middle = jnp.logical_not(rim)

    def fold_width(c, who):
        for kind in (GC_E, GC_W):
            copy, _, gets = build(kind, c, parts[c])
            pl.when(gets & who)(copy.wait_recv)

        @pl.when(who)
        def _():
            for h in range(*parts[c]):
                for t in range(2):
                    for ns in range(2):
                        for col in range(2):
                            both = acc[h, t, 4 + ns * 2 + col] + gwr[col, h, 2 + ns, t].astype(F32)
                            gh[ns, h, t, col] = both.astype(BF16)

        for kind in (GH_S, GH_N):
            copy, sends, _ = build(kind, c, parts[c])
            pl.when(sends & who)(copy.start)

    def fold_height(c):
        arrive(parts[c][1], GO_E, GO_W, GH_S, GH_N)
        for t, ref in enumerate((dk_ref, dv_ref)):
            both = []
            for h in range(*parts[c]):
                tiles = [
                    acc[h, t, r * 2 + col] + ghr[r, h, t, col].astype(F32) + gwr[col, h, r, t].astype(F32)
                    for r in range(2)
                    for col in range(2)
                ]
                both.append(jnp.concatenate(tiles, axis=0).astype(BF16))
            lo, width = parts[c][0] * size, len(both) * size
            grid = dot(back, jnp.concatenate(both, axis=1), NN)
            ref[:, :, :, lo : lo + width] = grid.reshape(2, 8, 8, width).astype(BF16)

    def forward(c):
        arrive(parts[c][1], Z_S, Z_N)
        begin(parts[c][1], C_E, C_W)
        begin(parts[c][1] + EARLY, W_E, W_W)

    for c in range(min(AHEAD, chunks)):
        forward(c)
    loads[7].wait()
    loads[8].wait()
    for step in range(chunks):
        if step + AHEAD < chunks:
            forward(step + AHEAD)
        arrive(parts[step][1], W_E, W_W, C_E, C_W)
        rest = [attend(h) for h in range(*parts[step])]
        begin(parts[step][1], GC_E, GC_W)
        for finish in rest:
            finish()
        if step >= BEHIND:
            fold_width(step - BEHIND, middle)
        if step >= NEAR:
            fold_width(step - NEAR, rim)
        begin(parts[step][1] - LATE, GO_E, GO_W)
    for c in range(max(chunks - NEAR, 0), chunks):
        fold_width(c, rim)
    for c in range(max(chunks - BEHIND, 0), chunks):
        fold_width(c, middle)
        begin(parts[c][1], GO_E, GO_W)
    for c in range(chunks):
        fold_height(c)

    for kind in range(KINDS):
        copy, sends, _ = build(kind, 0, (0, heads))
        pl.when(sends)(copy.wait_send)


def store(*refs):
    sem = refs[-1]
    count = len(refs) // 2
    copies = [
        pltpu.make_async_copy(refs[i], refs[count + i], sem.at[i]) for i in range(count)
    ]
    for copy in copies:
        copy.start()
    for copy in copies:
        copy.wait()


def local(n_ha, n_wa, queries, keys, values, out_grad, windows, valid_rows, valid_cols):
    heads = windows.shape[0]
    size = queries.shape[-1] // heads
    vmem = pl.BlockSpec(memory_space=pltpu.VMEM)
    hbm = pl.BlockSpec(memory_space=pltpu.HBM)
    shape = jax.ShapeDtypeStruct(queries.shape, BF16)
    held = [
        pltpu.with_memory_space_constraint(x, pltpu.HBM)
        for x in (queries, keys, values, out_grad, windows.T, valid_rows, valid_cols)
    ]
    results = pl.pallas_call(
        functools.partial(kernel, heads, n_ha, n_wa),
        out_shape=(shape,) * 4,
        in_specs=[hbm] * 7,
        out_specs=(vmem,) * 4,
        scratch_shapes=[pltpu.VMEM(queries.shape, BF16)] * 4
        + [
            pltpu.SMEM((4, heads), jnp.int32),
            pltpu.SMEM(valid_rows.shape, jnp.int32),
            pltpu.SMEM(valid_cols.shape, jnp.int32),
            pltpu.VMEM((heads, 2, 2, 2, 32, size), BF16),
            pltpu.VMEM((heads, 2, 2, 2, 32, size), BF16),
            pltpu.VMEM((2, heads, 4, 2, 32, size), BF16),
            pltpu.VMEM((2, heads, 4, 2, 32, size), BF16),
            pltpu.VMEM((2, heads, 4, 2, 32, size), BF16),
            pltpu.VMEM((2, heads, 2, 2, 32, size), BF16),
            pltpu.VMEM((2, heads, 2, 2, 32, size), BF16),
            pltpu.VMEM((heads, 2, 8, 32, size), F32),
            pltpu.VMEM((16, 32, 128), F32),
            pltpu.SemaphoreType.DMA((9,)),
            pltpu.SemaphoreType.REGULAR((2,)),
            pltpu.SemaphoreType.DMA((KINDS,)),
            pltpu.SemaphoreType.DMA((KINDS, heads)),
        ],
        compiler_params=pltpu.CompilerParams(
            collective_id=0, has_side_effects=True, vmem_limit_bytes=40 << 20
        ),
    )(*held)
    return pl.pallas_call(
        store,
        out_shape=(shape,) * 4,
        in_specs=[pl.BlockSpec(memory_space=pl.ANY)] * 4,
        out_specs=(hbm,) * 4,
        scratch_shapes=[pltpu.SemaphoreType.DMA((4,))],
        compiler_params=pltpu.CompilerParams(vmem_limit_bytes=1 << 20),
    )(*results)


def solution(mesh):
    cells = P("clip", "ha", "wa", None)
    body = functools.partial(local, mesh.shape["ha"], mesh.shape["wa"])
    return jax.shard_map(
        body,
        mesh=mesh,
        in_specs=(cells,) * 4 + (P(),) * 3,
        out_specs=(cells,) * 4,
        check_vma=False,
    )
```

```python
import functools
import math

import jax
import jax.numpy as jnp
from jax import lax
from jax.experimental import pallas as pl
from jax.experimental.pallas import tpu as pltpu
from jax.sharding import PartitionSpec as P

TILE = 4
SIZES = (1,) * 12
NEG = -1e30
LOG2E = math.log2(math.e)
MESH = pl.DeviceIdType.MESH
F32 = jnp.float32
BF16 = jnp.bfloat16

KINDS = 12
Z_S, Z_N, W_E, W_W, C_E, C_W, GC_E, GC_W, GO_E, GO_W, GH_S, GH_N = range(KINDS)
EARLY = 9
AHEAD = 4
BEHIND = 4
NEAR = 3
FIRST = 2
LATE = 8
MEET = 2
WIDE = (1,) * 12
OWNS = (1,) * 12
TILES = (
    (1, 1), (1, 2), (2, 1), (2, 2), (0, 1), (0, 2), (3, 1), (3, 2),
    (1, 0), (2, 0), (1, 3), (2, 3), (0, 0), (3, 0), (0, 3), (3, 3),
)


def split(heads, sizes):
    edges = [0]
    for size in sizes:
        edges.append(min(edges[-1] + size, heads))
    edges += range(edges[-1] + 1, heads + 1)
    return [(a, b) for a, b in zip(edges, edges[1:]) if b > a]


def iota(shape, dim):
    return lax.broadcasted_iota(jnp.int32, shape, dim)


def native_of(a):
    tr, tc, f, r, c = a >> 6, (a >> 5) & 1, (a >> 4) & 1, (a >> 2) & 3, a & 3
    return f * 64 + (tr * 4 + r) * 8 + tc * 4 + c


def dot(a, b, dims):
    return lax.dot_general(a, b, (dims, ((), ())), preferred_element_type=F32)


NT = ((1,), (1,))
NN = ((1,), (0,))
TN = ((0,), (0,))


def kernel(
    heads, n_ha, n_wa,
    q_hbm, k_hbm, v_hbm, g_hbm, win_hbm, vr_hbm, vc_hbm,
    att_ref, dq_ref, dk_ref, dv_ref,
    q_ref, k_ref, v_ref, g_ref, win_ref, vr_ref, vc_ref, own, zin, win, gw, gwr, gh, ghr, acc, kb, load, ready, send, recv,
):
    size = own.shape[-1]
    parts = split(heads, SIZES)
    chunks = len(parts)
    scale = 1.0 / math.sqrt(size)
    ha, wa = lax.axis_index("ha"), lax.axis_index("wa")
    has_n, has_s = ha > 0, ha < n_ha - 1
    has_w, has_e = wa > 0, wa < n_wa - 1
    to_n, to_s = {"ha": ha - 1}, {"ha": ha + 1}
    to_w, to_e = {"wa": wa - 1}, {"wa": wa + 1}

    cut = FIRST * size
    feats = q_ref.shape[-1]

    def lanes(src, dst, lo, hi):
        at = (slice(None), slice(None), slice(None), slice(lo, hi))
        return src.at[at], dst.at[at]

    loads = [
        pltpu.make_async_copy(src, dst, load.at[i])
        for i, (src, dst) in enumerate(
            (
                lanes(k_hbm, k_ref, 0, cut), lanes(v_hbm, v_ref, 0, cut),
                lanes(k_hbm, k_ref, cut, feats), lanes(v_hbm, v_ref, cut, feats),
                (win_hbm, win_ref), (vr_hbm, vr_ref), (vc_hbm, vc_ref),
                (q_hbm, q_ref), (g_hbm, g_ref),
            )
        )
    ]
    for copy in loads:
        copy.start()

    barrier = pltpu.get_barrier_semaphore()
    for has, to in ((has_s, to_s), (has_e, to_e)):

        @pl.when(has)
        def _():
            pl.semaphore_signal(barrier, inc=1, device_id=to, device_id_type=MESH)

    @pl.when(has_n | has_w)
    def _():
        pl.semaphore_wait(barrier, has_n.astype(jnp.int32) + has_w.astype(jnp.int32))

    for i, (has, to) in enumerate(((has_n, to_n), (has_w, to_w))):

        @pl.when(has)
        def _():
            pl.semaphore_signal(ready.at[i], inc=1, device_id=to, device_id_type=MESH)

    cells = 128
    perm = jnp.where(native_of(iota((cells, cells), 0)) == iota((cells, cells), 1), 1.0, 0.0)
    perm = perm.astype(BF16)
    back = jnp.where(native_of(iota((cells, cells), 1)) == iota((cells, cells), 0), 1.0, 0.0)
    back = back.astype(BF16)

    def flat(ref, lo, width):
        return ref[:, :, :, lo : lo + width].astype(F32).reshape(cells, width).astype(BF16)

    def permute(c):
        first, last = parts[c]
        for t, ref in enumerate((k_ref, v_ref)):
            width = (last - first) * size
            tiles = dot(perm, flat(ref, first * size, width), NN).astype(BF16)
            for h in range(first, last):
                lo = (h - first) * size
                own[h, :, t] = tiles[:, lo : lo + size].reshape(2, 2, 32, size)

    routes = {
        "n": (to_n, has_n, has_s), "s": (to_s, has_s, has_n),
        "w": (to_w, has_w, has_e), "e": (to_e, has_e, has_w),
    }
    half = {GO_E: slice(0, 2), GO_W: slice(0, 2), GC_E: slice(2, 4), GC_W: slice(2, 4)}

    def ends(kind, at):
        if kind == Z_S:
            return "s", own.at[at, 1], zin.at[at, 0]
        if kind == Z_N:
            return "n", own.at[at, 0], zin.at[at, 1]
        if kind == W_E:
            return "e", own.at[at, :, :, 1], win.at[0, at, 0:2]
        if kind == W_W:
            return "w", own.at[at, :, :, 0], win.at[1, at, 0:2]
        if kind == C_E:
            return "e", zin.at[at, :, :, 1], win.at[0, at, 2:4]
        if kind == C_W:
            return "w", zin.at[at, :, :, 0], win.at[1, at, 2:4]
        if kind in (GC_E, GO_E):
            return "e", gw.at[1, at, half[kind]], gwr.at[0, at, half[kind]]
        if kind in (GC_W, GO_W):
            return "w", gw.at[0, at, half[kind]], gwr.at[1, at, half[kind]]
        if kind == GH_S:
            return "s", gh.at[1, at], ghr.at[0, at]
        return "n", gh.at[0, at], ghr.at[1, at]

    def build(kind, c, part):
        way, src, dst = ends(kind, slice(*part))
        to, sends, gets = routes[way]
        copy = pltpu.make_async_remote_copy(
            src_ref=src, dst_ref=dst, send_sem=send.at[kind], recv_sem=recv.at[kind, c],
            device_id=to, device_id_type=MESH,
        )
        return copy, sends, gets

    cuts = {kind: parts for kind in range(KINDS)}
    cuts[W_E] = cuts[W_W] = split(heads, WIDE)
    cuts[GO_E] = cuts[GO_W] = split(heads, OWNS)
    begun, ended = [0] * KINDS, [0] * KINDS

    def begin(last, *kinds):
        for kind in kinds:
            while begun[kind] < len(cuts[kind]) and cuts[kind][begun[kind]][1] <= last:
                copy, sends, _ = build(kind, begun[kind], cuts[kind][begun[kind]])
                pl.when(sends)(copy.start)
                begun[kind] += 1

    def arrive(last, *kinds):
        for kind in kinds:
            while ended[kind] < len(cuts[kind]) and cuts[kind][ended[kind]][0] < last:
                copy, _, gets = build(kind, ended[kind], cuts[kind][ended[kind]])
                pl.when(gets)(copy.wait_recv)
                ended[kind] += 1

    loads[0].wait()
    loads[1].wait()
    for c in range(chunks):
        if c == FIRST:
            loads[2].wait()
            loads[3].wait()
        permute(c)
        begin(parts[c][1], Z_N)
        begin(min(parts[c][1], EARLY), W_W)
        if c == min(MEET, chunks) - 1:
            for i, has in enumerate((has_s, has_e)):

                @pl.when(has)
                def _():
                    pl.semaphore_wait(ready.at[i], 1)

        if c >= min(MEET, chunks) - 1:
            begin(parts[c][1], Z_S)
            begin(min(parts[c][1], EARLY), W_E)

    def clear(has, ref, *index):
        @pl.when(jnp.logical_not(has))
        def _():
            view = ref.at[index]
            view[...] = jnp.zeros(view.shape, ref.dtype)

    every = slice(None)
    clear(has_n, zin, every, 0)
    clear(has_s, zin, every, 1)
    clear(has_w, win, 0)
    clear(has_e, win, 1)
    clear(has_w, gwr, 0)
    clear(has_e, gwr, 1)
    clear(has_n, ghr, 0)
    clear(has_s, ghr, 1)

    for copy in loads[4:7]:
        copy.wait()

    def limits(ref, first):
        count = ref.shape[0]
        out = []
        for e in range(4):
            at = first + e
            inside = (at >= 0) & (at < count)
            out.append(jnp.where(inside, ref[jnp.clip(at, 0, count - 1)], 0))
        return out

    rows, cols = limits(vr_ref, ha * 2 - 1), limits(vc_ref, wa * 2 - 1)
    lane = iota((1, cells), 1)
    lane_r, lane_c = (lane >> 3) & 7, lane & 7
    tile_r, tile_c = (lane_r >> 2) + 1, (lane_c >> 2) + 1
    live = ((lane_r & 3) < jnp.where(tile_r == 1, rows[1], rows[2])) & (
        (lane_c & 3) < jnp.where(tile_c == 1, cols[1], cols[2])
    )
    live = jnp.where(live, 1.0, 0.0).astype(F32)
    sub = iota((32, cells), 0)
    for t, (er, ec) in enumerate(TILES):
        ok = (((sub >> 2) & 3) < rows[er]) & ((sub & 3) < cols[ec])
        kb[t] = jnp.where(ok, 0.0, NEG)

    def attend(h):
        lo = h * size
        w = [win_ref[j, h] for j in range(4)]
        row_bias = [
            jnp.where((e - tile_r >= -w[0]) & (e - tile_r <= w[1]), 0.0, NEG) for e in range(4)
        ]
        col_bias = [
            jnp.where((e - tile_c >= -w[2]) & (e - tile_c <= w[3]), 0.0, NEG) for e in range(4)
        ]
        q = flat(q_ref, lo, size)
        g = flat(g_ref, lo, size)
        key, val = (
            jnp.concatenate(
                [
                    own[h, :, t].reshape(128, size), zin[h, :, t].reshape(128, size),
                    win[0, h, 0:2, t].reshape(64, size), win[1, h, 0:2, t].reshape(64, size),
                    win[0, h, 2:4, t].reshape(64, size), win[1, h, 2:4, t].reshape(64, size),
                ],
                axis=0,
            )
            for t in range(2)
        )
        raw = dot(key, q, NT)
        s = [
            raw[t * 32 : t * 32 + 32] * (scale * LOG2E) + (kb[t] + (row_bias[er] + col_bias[ec]))
            for t, (er, ec) in enumerate(TILES)
        ]
        top = jnp.max(functools.reduce(jnp.maximum, s), axis=0, keepdims=True)
        e = [jnp.exp2(x - top) for x in s]
        total = jnp.sum(sum(e[1:], e[0]), axis=0, keepdims=True)
        inv = live / total
        p = [x * inv for x in e]
        low = [x.astype(BF16) for x in p]
        low_all = jnp.concatenate(low, axis=0)
        raw_d = dot(val, g, NT)
        dp = [raw_d[t * 32 : t * 32 + 32] for t in range(16)]
        prod = [a.astype(F32) * b for a, b in zip(low, dp)]
        dots = jnp.sum(sum(prod[1:], prod[0]), axis=0, keepdims=True)
        ds = jnp.concatenate([(a * (b - dots)).astype(BF16) for a, b in zip(p, dp)], axis=0)
        for t, (left, right) in enumerate(((ds, q), (low_all, g))):
            part = dot(left[384:512], right, NN)
            if t == 0:
                part = part * scale
            part = part.reshape(2, 2, 32, size).astype(BF16)
            for side in range(2):
                gw[side, h, 2:4, t] = part[side]

        def finish():
            for t, (left, right) in enumerate(((ds, q), (low_all, g))):
                part = dot(left[0:384], right, NN)
                if t == 0:
                    part = part * scale
                acc[h, t] = part[0:256].reshape(8, 32, size)
                for side in range(2):
                    rim = part[256 + side * 64 : 320 + side * 64]
                    gw[side, h, 0:2, t] = rim.reshape(2, 32, size).astype(BF16)
            out = dot(low_all, val, TN)
            att_ref[:, :, :, lo : lo + size] = out.reshape(2, 8, 8, size).astype(BF16)
            dq = dot(ds, key, TN) * scale
            dq_ref[:, :, :, lo : lo + size] = dq.reshape(2, 8, 8, size).astype(BF16)

        return finish

    rim = (wa == 0) | (wa == n_wa - 1)
    middle = jnp.logical_not(rim)

    def fold_width(c, who):
        for kind in (GC_E, GC_W):
            copy, _, gets = build(kind, c, parts[c])
            pl.when(gets & who)(copy.wait_recv)

        @pl.when(who)
        def _():
            for h in range(*parts[c]):
                for t in range(2):
                    for ns in range(2):
                        for col in range(2):
                            both = acc[h, t, 4 + ns * 2 + col] + gwr[col, h, 2 + ns, t].astype(F32)
                            gh[ns, h, t, col] = both.astype(BF16)

        for kind in (GH_S, GH_N):
            copy, sends, _ = build(kind, c, parts[c])
            pl.when(sends & who)(copy.start)

    def fold_height(c):
        arrive(parts[c][1], GO_E, GO_W, GH_S, GH_N)
        for t, ref in enumerate((dk_ref, dv_ref)):
            both = []
            for h in range(*parts[c]):
                tiles = [
                    acc[h, t, r * 2 + col] + ghr[r, h, t, col].astype(F32) + gwr[col, h, r, t].astype(F32)
                    for r in range(2)
                    for col in range(2)
                ]
                both.append(jnp.concatenate(tiles, axis=0).astype(BF16))
            lo, width = parts[c][0] * size, len(both) * size
            grid = dot(back, jnp.concatenate(both, axis=1), NN)
            ref[:, :, :, lo : lo + width] = grid.reshape(2, 8, 8, width).astype(BF16)

    def forward(c):
        arrive(parts[c][1], Z_S, Z_N)
        begin(parts[c][1], C_E, C_W)
        begin(parts[c][1] + EARLY, W_E, W_W)

    for c in range(min(AHEAD, chunks)):
        forward(c)
    loads[7].wait()
    loads[8].wait()
    for step in range(chunks):
        if step + AHEAD < chunks:
            forward(step + AHEAD)
        arrive(parts[step][1], W_E, W_W, C_E, C_W)
        rest = [attend(h) for h in range(*parts[step])]
        begin(parts[step][1], GC_E, GC_W)
        for finish in rest:
            finish()
        if step >= BEHIND:
            fold_width(step - BEHIND, middle)
        if step >= NEAR:
            fold_width(step - NEAR, rim)
        begin(parts[step][1] - LATE, GO_E, GO_W)
    for c in range(max(chunks - NEAR, 0), chunks):
        fold_width(c, rim)
    for c in range(max(chunks - BEHIND, 0), chunks):
        fold_width(c, middle)
        begin(parts[c][1], GO_E, GO_W)
    for c in range(chunks):
        fold_height(c)

    for kind in range(KINDS):
        copy, sends, _ = build(kind, 0, (0, heads))
        pl.when(sends)(copy.wait_send)


def store(*refs):
    sem = refs[-1]
    count = len(refs) // 2
    copies = [
        pltpu.make_async_copy(refs[i], refs[count + i], sem.at[i]) for i in range(count)
    ]
    for copy in copies:
        copy.start()
    for copy in copies:
        copy.wait()


def local(n_ha, n_wa, queries, keys, values, out_grad, windows, valid_rows, valid_cols):
    heads = windows.shape[0]
    size = queries.shape[-1] // heads
    vmem = pl.BlockSpec(memory_space=pltpu.VMEM)
    hbm = pl.BlockSpec(memory_space=pltpu.HBM)
    shape = jax.ShapeDtypeStruct(queries.shape, BF16)
    held = [
        pltpu.with_memory_space_constraint(x, pltpu.HBM)
        for x in (queries, keys, values, out_grad, windows.T, valid_rows, valid_cols)
    ]
    results = pl.pallas_call(
        functools.partial(kernel, heads, n_ha, n_wa),
        out_shape=(shape,) * 4,
        in_specs=[hbm] * 7,
        out_specs=(vmem,) * 4,
        scratch_shapes=[pltpu.VMEM(queries.shape, BF16)] * 4
        + [
            pltpu.SMEM((4, heads), jnp.int32),
            pltpu.SMEM(valid_rows.shape, jnp.int32),
            pltpu.SMEM(valid_cols.shape, jnp.int32),
            pltpu.VMEM((heads, 2, 2, 2, 32, size), BF16),
            pltpu.VMEM((heads, 2, 2, 2, 32, size), BF16),
            pltpu.VMEM((2, heads, 4, 2, 32, size), BF16),
            pltpu.VMEM((2, heads, 4, 2, 32, size), BF16),
            pltpu.VMEM((2, heads, 4, 2, 32, size), BF16),
            pltpu.VMEM((2, heads, 2, 2, 32, size), BF16),
            pltpu.VMEM((2, heads, 2, 2, 32, size), BF16),
            pltpu.VMEM((heads, 2, 8, 32, size), F32),
            pltpu.VMEM((16, 32, 128), F32),
            pltpu.SemaphoreType.DMA((9,)),
            pltpu.SemaphoreType.REGULAR((2,)),
            pltpu.SemaphoreType.DMA((KINDS,)),
            pltpu.SemaphoreType.DMA((KINDS, heads)),
        ],
        compiler_params=pltpu.CompilerParams(
            collective_id=0, has_side_effects=True, vmem_limit_bytes=40 << 20
        ),
    )(*held)
    return pl.pallas_call(
        store,
        out_shape=(shape,) * 4,
        in_specs=[pl.BlockSpec(memory_space=pl.ANY)] * 4,
        out_specs=(hbm,) * 4,
        scratch_shapes=[pltpu.SemaphoreType.DMA((4,))],
        compiler_params=pltpu.CompilerParams(vmem_limit_bytes=1 << 20),
    )(*results)


def solution(mesh):
    cells = P("clip", "ha", "wa", None)
    body = functools.partial(local, mesh.shape["ha"], mesh.shape["wa"])
    return jax.shard_map(
        body,
        mesh=mesh,
        in_specs=(cells,) * 4 + (P(),) * 3,
        out_specs=(cells,) * 4,
        check_vma=False,
    )
```
